128 devices in a mesh: fibre: 8 (over z, core), blk: 16 (over x, y).
Axes of the slice: x: 4, y: 4, z: 4, core: 2. Of those that a mesh axis runs over, the one named last changes fastest.
Arguments:
- readings: bfloat16 [524288, 1024], P(('fibre', 'blk')), as said below
- values: bfloat16 [524288], P(('fibre', 'blk')), may hold values from -6 to 6
- counts: int32 [128], P(('fibre', 'blk')), may hold values from 1 to 4096, as said below
- prior_root: float32 [1024, 1024], P(('fibre', 'blk')), as said below
- prior_info: float32 [1024], P(('fibre', 'blk')), may hold values from -6 to 6
Outputs:
- post_root: float32 [1024, 1024], P('blk')
- post_info: float32 [1024], replicated
The draws below stay inside these ranges and needn't reach their ends.
Inputs may be any that keep to these rules, and one draw needn't show every extreme that they name: `counts`: every owner has at least one live row, and in every draw some owner has all 4096 rows live. `prior_root`: upper triangular with a positive diagonal. `readings`: whitened measurement rows; nothing beyond the stated range is promised.
All inputs are finite; a program needn't handle non-finite values.
Results may differ from the reference program's by a relative error of at most 0.0003.
Values sent between devices are 32-bit elements; how exact they have to be, the bound alone decides.
A program may use at most 128 MiB of HBM per device.

```python
import jax
import jax.numpy as jnp
from jax import lax

NS = 1024
CAP = 4096
OWNERS = 128


def draw_counts(key, part):
    first_key, second_key = jax.random.split(jax.random.fold_in(key, 11))
    drawn = jax.random.randint(first_key, (OWNERS,), CAP // 8, CAP + 1)
    fullest = jax.random.randint(second_key, (), 0, OWNERS)
    return jnp.where(jnp.arange(OWNERS) == fullest, CAP, drawn).astype(jnp.int32)


def draw_prior_root(key, part):
    first_key, second_key = jax.random.split(jax.random.fold_in(key, 23))
    diagonal = jax.random.uniform(first_key, (NS,), jnp.float32, 1.0, 2.0)
    spread_part = jax.random.normal(second_key, (NS, NS), jnp.float32) * (0.7 / NS ** 0.5)
    places = jnp.arange(NS)
    upper_mask = places[:, None] < places[None, :]
    return jnp.where(upper_mask, spread_part, 0.0) + jnp.diag(diagonal)


def draw_readings(key, part):
    mix_key, row_key = jax.random.split(jax.random.fold_in(key, 37))
    coupling_key, left_key, right_key = jax.random.split(mix_key, 3)
    coupling_scale = 0.6 / NS ** 0.5
    row_scale = (2.0 / (CAP * OWNERS)) ** 0.5
    mode_count = 4
    coupling = jnp.clip(jax.random.normal(coupling_key, (NS, NS), jnp.float32), -3.0, 3.0) * coupling_scale
    left_modes = jnp.clip(jax.random.normal(left_key, (mode_count, NS), jnp.float32), -4.0, 4.0) * (1.0 / NS ** 0.5)
    right_modes = jnp.clip(jax.random.normal(right_key, (mode_count, NS), jnp.float32), -4.0, 4.0) * (40.0 / NS) ** 0.5
    common = jnp.dot(left_modes.T, right_modes, precision=lax.Precision.HIGHEST)
    mixing = coupling + common + jnp.eye(NS, dtype=jnp.float32)

    def one_owner(owner):
        owner_key = jax.random.fold_in(row_key, owner)
        white_key = jax.random.fold_in(owner_key, 0)
        white = jnp.clip(jax.random.normal(white_key, (CAP, NS), jnp.float32), -6.0, 6.0)
        mixed = jnp.dot(white, mixing, precision=lax.Precision.HIGHEST) * row_scale
        return mixed.astype(jnp.bfloat16)
    blocks = lax.map(one_owner, jnp.arange(OWNERS, dtype=jnp.int32))
    return blocks.reshape(OWNERS * CAP, NS)


def steps_of(rng, extent, shards, least, high):
    def one(axis_at, parts):
        steps = jax.random.uniform(jax.random.fold_in(jax.random.fold_in(rng, 6), axis_at), (parts,), jnp.float32, least / len(shards), high / len(shards))
        return jnp.repeat(jnp.exp(steps), extent[axis_at] // parts).reshape((-1,) + (1,) * (len(extent) - axis_at - 1))

    level = one(*shards[0])
    for cut in shards[1:]:
        level = level * one(*cut)
    return level


def normal_values(rng, extent, width, limit, cuts=(), held_as=jnp.bfloat16):
    level = steps_of(rng, extent, cuts, -0.22, 0.18) if cuts else 1.0
    array = jax.random.normal(rng, extent, jnp.float32) * width * level
    return jnp.minimum(jnp.maximum(array, -limit), limit).astype(held_as)


def setup_inputs(seed: int = 0) -> dict:
    keys = jax.random.split(jax.random.key(seed), 6)
    readings = draw_readings(jax.random.fold_in(keys[5], 71), 0)
    values = normal_values(keys[1], (OWNERS * CAP,), 1.0, 6.0, ((0, 128),))
    counts = draw_counts(jax.random.fold_in(keys[5], 71), 0)
    prior_root = draw_prior_root(jax.random.fold_in(keys[5], 71), 0)
    prior_info = normal_values(keys[4], (NS,), 1.0, 6.0, ((0, 128),), jnp.float32)
    return {"readings": readings, "values": values, "counts": counts, "prior_root": prior_root, "prior_info": prior_info}


def reference(readings, values, counts, prior_root, prior_info):
    owner_rows = readings.reshape(OWNERS, CAP, NS)
    owner_vals = values.reshape(OWNERS, CAP)
    positions = jnp.arange(CAP, dtype=jnp.int32)

    def add_owner(totals, owner_item):
        row_block, val_block, count_one = owner_item
        live_mask = positions < count_one
        row_block = jnp.where(live_mask[:, None], row_block, jnp.zeros((), row_block.dtype))
        val_block = jnp.where(live_mask, val_block, jnp.zeros((), val_block.dtype))
        gram_part = lax.dot_general(row_block.astype(jnp.float32), row_block.astype(jnp.float32), (((0,), (0,)), ((), ())), preferred_element_type=jnp.float32)
        info_part = jnp.dot(val_block.astype(jnp.float32), row_block.astype(jnp.float32), preferred_element_type=jnp.float32)
        return ((totals[0] + gram_part, totals[1] + info_part), None)
    initial = (jnp.zeros((NS, NS), jnp.float32), jnp.zeros((NS,), jnp.float32))
    totals, unused_out = lax.scan(add_owner, initial, (owner_rows, owner_vals, counts))
    gram_sum = totals[0] + jnp.dot(prior_root.T, prior_root, precision=lax.Precision.HIGHEST)
    info_sum = totals[1] + jnp.dot(prior_info, prior_root, precision=lax.Precision.HIGHEST)
    factor = jnp.linalg.cholesky(gram_sum)
    post_info = lax.linalg.triangular_solve(factor, info_sum[:, None], left_side=True, lower=True)[:, 0]
    return (factor.T, post_info)
```

```python
import jax, jax.numpy as jnp, numpy as np
from jax import lax
from jax.experimental import pallas as pl
from jax.experimental.pallas import tpu as pltpu
F32=jnp.float32
def bc(x,shape): return jnp.broadcast_to(x,shape)

def factor_block(T, n=16, W=256):
    out=[]
    sub=lax.broadcasted_iota(jnp.int32,(8,128),0)
    for p in range(n):
        V=T[p]
        C=[bc(V[:,8*p+c:8*p+c+1],(8,128)) for c in range(8)]
        Q={q:[bc(T[q][:,8*p+c:8*p+c+1],(8,128)) for c in range(8)] for q in range(p+1,n)}
        Vp=[V[:,128*w:128*w+128] for w in range(W//128)]
        rv=jnp.zeros((8,128),F32)
        rs=[];
        LQ={q:[] for q in Q}
        rows=[]
        for j in range(8):
            d=bc(C[j][j:j+1,:],(8,128))
            r=lax.rsqrt(d)
            L=C[j]*r
            Lm=jnp.where(sub>j,L,0.0) if j<7 else None
            rv=jnp.where(sub==j,r,rv)
            Rj=[bc(v[j:j+1,:],(8,128))*r for v in Vp]
            rows.append(Rj)
            if j<7:
                Vp=[v-Lm*rj for v,rj in zip(Vp,Rj)]
                Ls={k:bc(L[k:k+1,:],(8,128)) for k in range(j+1,8)}
                for k in range(j+1,8): C[k]=C[k]-L*Ls[k]
            for q in Q:
                Lq=Q[q][j]*r
                LQ[q].append(Lq)
                if j<7:
                    for k in range(j+1,8): Q[q][k]=Q[q][k]-Lq*Ls[k]
        out.append(jnp.concatenate([v*rv for v in Vp],axis=1))
        for q in Q:
            parts=[T[q][:,128*w:128*w+128] for w in range(W//128)]
            for j in range(8):
                parts=[a-LQ[q][j]*rj for a,rj in zip(parts,rows[j])]
            T[q]=jnp.concatenate(parts,axis=1)
    return out
BF=jnp.bfloat16
def split3(x):
    h=x.astype(BF); r=x-h.astype(F32); m=r.astype(BF); l=(r-m.astype(F32)).astype(BF)
    return h,m,l
def lhs6(x):
    h,m,l=split3(x); return jnp.concatenate([h,h,m,m,h,l],axis=1)
def rhs6(x):
    h,m,l=split3(x); return jnp.concatenate([h,m,h,m,l,h],axis=0)
def bidx(k,j): return 8*k-k*(k-1)//2+(j-k)
def chol_kernel(a_ref,b_ref,r_ref,y_ref,A,*,fac=factor_block):
    A[...]=a_ref[...]
    b=b_ref[...]
    ii=lax.broadcasted_iota(jnp.int32,(8,128),0); jj=lax.broadcasted_iota(jnp.int32,(8,128),1)
    def blk(k,j): return pl.ds(brow(bidx(k,j)),128)
    bl=[b[k:k+1,:] for k in range(8)]
    for k in range(8):
        o=brow(bidx(k,k))
        T=[jnp.concatenate([A[o+8*p:o+8*p+8,:],jnp.where(jj==ii+8*p,1.0,0.0).astype(F32)],axis=1) for p in range(16)]
        out=fac(T)
        for p in range(16): r_ref[128*k+8*p:128*k+8*p+8,128*k:128*k+128]=jnp.where(jj>=ii+8*p,out[p][:,:128],0.0)
        if k: r_ref[128*k:128*k+128,:128*k]=jnp.zeros((128,128*k),F32)
        Linv=jnp.concatenate([t[:,128:] for t in out],axis=0)
        bk=jnp.concatenate([bl[k],jnp.zeros((7,128),F32)],axis=0)
        yk=lax.dot_general(bk,Linv,(((1,),(1,)),((),())),precision=lax.Precision.HIGHEST,preferred_element_type=F32)
        y_ref[k:k+1,:]=yk[0:1,:]
        n=7-k
        if n==0: break
        row=jnp.concatenate([A[blk(k,j),:] for j in range(k+1,8)],axis=1)
        R=jnp.dot(lhs6(Linv),rhs6(row),preferred_element_type=F32)
        r_ref[128*k:128*k+128,128*(k+1):]=R
        X=jnp.concatenate([lhs6(R[:,128*i:128*i+128].T) for i in range(n)]+[lhs6(jnp.concatenate([yk,jnp.zeros((8,128),F32)],axis=0))],axis=0)
        Y=rhs6(R)
        for c in range(0,n,2):
            w=min(2,n-c)
            rows=128*(c+w)
            D=jnp.dot(jnp.concatenate([X[128*n:],X[:rows]],axis=0),Y[:,128*c:128*(c+w)],preferred_element_type=F32)
            for u in range(w):
                j=k+1+c+u
                bl[j]=bl[j]-D[0:1,128*u:128*u+128]
                for i in range(k+1,j+1):
                    z=16+128*(i-k-1)
                    A[blk(i,j),:]=A[blk(i,j),:]-D[z:z+128,128*u:128*u+128]
def chol_call(a,b,fac=factor_block):
    import functools
    return pl.pallas_call(functools.partial(chol_kernel,fac=fac),out_shape=(jax.ShapeDtypeStruct((1024,1024),F32),jax.ShapeDtypeStruct((8,128),F32)),
      scratch_shapes=[pltpu.VMEM((ROWS,128),F32)],compiler_params=pltpu.CompilerParams(vmem_limit_bytes=56*2**20))(a,b)
NS=1024; CAP=4096
CH=1024
def brow(i): return 128*i if i<12 else 128*i+256
INFO=1536
ROWS=4864
def gram_kernel(cnt_ref,pi_ref,x_ref,v_ref,pr_ref,g_ref):
    s=pl.program_id(0)
    x=x_ref[...]
    rowi=lax.broadcasted_iota(jnp.int32,(CH,NS),0)+s*CH
    xm=jnp.where(rowi<cnt_ref[0],x,jnp.zeros((),BF))
    xt=x.T
    v=jnp.broadcast_to(v_ref[...],(16,CH))
    def accum(first,xt,v,xm):
        lhs=jnp.concatenate([v,xt],axis=0)
        for c in range(4):
            D=lax.dot_general(lhs[:16+256*(c+1)],xm[:,256*c:256*c+256],(((1,),(0,)),((),())),preferred_element_type=F32)
            for u in range(2):
                j=2*c+u
                dv=D[0:1,128*u:128*u+128]
                if first: g_ref[INFO+j:INFO+j+1,:]=dv
                else: g_ref[INFO+j:INFO+j+1,:]=g_ref[INFO+j:INFO+j+1,:]+dv
                for i in range(j+1):
                    z=16+128*i; o=brow(bidx(i,j))
                    if first: g_ref[o:o+128,:]=D[z:z+128,128*u:128*u+128]
                    else: g_ref[o:o+128,:]=g_ref[o:o+128,:]+D[z:z+128,128*u:128*u+128]
    @pl.when(s==0)
    def _():
        accum(True,xt,v,xm)
        g_ref[INFO+8:INFO+256,:]=jnp.zeros((248,128),F32)
    @pl.when(s>0)
    def _(): accum(False,xt,v,xm)
    @pl.when(s==pl.num_programs(0)-1)
    def _():
        sub=lax.broadcasted_iota(jnp.int32,(8,128),0)
        pv=jnp.zeros((8,128),F32)
        for i in range(8): pv=jnp.where(sub==i,pi_ref[i],pv)
        pr=jnp.concatenate([pr_ref[...],pv],axis=1)
        h,m,l=split3(pr)
        h,m,l=[t.astype(F32) for t in (h,m,l)]
        z=jnp.zeros((80,NS+128),F32)
        a=jnp.concatenate([h,h,m,m,h,l,z],axis=0)
        b=jnp.concatenate([h,m,h,m,l,h,z],axis=0)[:,:NS].astype(BF)
        at=a.T.astype(BF)
        accum(False,at[:NS],at[NS:NS+16],b)
def gram_call(counts,prior_info,readings,values,prior_root):
    return pl.pallas_call(gram_kernel,grid=(CAP//CH,),
        in_specs=[pl.BlockSpec(memory_space=pltpu.SMEM),pl.BlockSpec(memory_space=pltpu.SMEM),
                  pl.BlockSpec((CH,NS),lambda s:(s,0)),pl.BlockSpec((1,CH),lambda s:(0,s)),
                  pl.BlockSpec((8,NS),lambda s:(0,0))],
        out_specs=pl.BlockSpec((ROWS,128),lambda s:(0,0)),
        out_shape=jax.ShapeDtypeStruct((ROWS,128),F32),
        compiler_params=pltpu.CompilerParams(vmem_limit_bytes=56*2**20))(counts,prior_info,readings,values.reshape(1,CAP),prior_root)
MESH=pl.DeviceIdType.MESH
CHUNKS=((0,1792),(1792,1536),(3328,1536))
DIMS=((0,1,2),(1,2,0),(2,0,1))
def comm_kernel(g_ref,a_ref,*scr):
    (r0,r1,r2,p0,p1,p2,ssem,rsem)=(scr[0:3],scr[3:6],scr[6:9],scr[9:12],scr[12:15],scr[15:18],scr[18],scr[19])
    f=lax.axis_index("fibre"); q=lax.axis_index("blk")
    core=f%2; co=(q//4,q%4,f//2)
    def peer(dim,d):
        c=list(co); c[dim]=(c[dim]+d)%4
        return (c[2]*2+core,c[0]*4+c[1])
    partner=(co[2]*2+(1-core),q)
    bar=pltpu.get_barrier_semaphore()
    pl.semaphore_signal(bar,inc=1,device_id=partner,device_id_type=MESH)
    for dim in range(3):
        for d in range(1,4):
            pl.semaphore_signal(bar,inc=1,device_id=peer(dim,d),device_id_type=MESH)
    pl.semaphore_wait(bar,10)
    cnt=[0]
    def send(src,dst,dev):
        i=cnt[0]; cnt[0]+=1
        c=pltpu.make_async_remote_copy(src_ref=src,dst_ref=dst,send_sem=ssem.at[i],recv_sem=rsem.at[i],device_id=dev,device_id_type=MESH)
        c.start(); return c
    al=lambda v: pl.multiple_of(v,8)
    H=[n//2 for _,n in CHUNKS]
    cs=[]
    for c,(b,n) in enumerate(CHUNKS):
        cs.append(send(g_ref.at[pl.ds(al(b+(1-core)*H[c]),H[c])],r0[c],partner))
    st=[]
    for c,(b,n) in enumerate(CHUNKS):
        cs[c].wait()
        p0[c][...]=g_ref[pl.ds(al(b+core*H[c]),H[c]),:]+r0[c][...]
        Q=H[c]//4; dim=DIMS[c][0]
        st.append([send(p0[c].at[pl.ds(al(((co[dim]+d)%4)*Q),Q)],r1[c].at[d-1],peer(dim,d)) for d in range(1,4)])
    st2=[]
    for c in range(3):
        for x in st[c]: x.wait()
        Q=H[c]//4; dim=DIMS[c][0]
        p1[c][...]=(p0[c][pl.ds(al(co[dim]*Q),Q),:]+r1[c][0])+(r1[c][1]+r1[c][2])
        Q2=Q//4; dim=DIMS[c][1]
        st2.append([send(p1[c].at[pl.ds(al(((co[dim]+d)%4)*Q2),Q2)],r2[c].at[d-1],peer(dim,d)) for d in range(1,4)])
    st3=[]
    for c in range(3):
        for x in st2[c]: x.wait()
        Q2=H[c]//16; dim=DIMS[c][1]; dz=DIMS[c][2]
        me=co[dz]
        p2[c][me]=(p1[c][pl.ds(al(co[dim]*Q2),Q2),:]+r2[c][0])+(r2[c][1]+r2[c][2])
        st3.append([send(p2[c].at[me],p2[c].at[me],peer(dz,d)) for d in range(1,4)])
    st4=[]
    def off(c,lvl):
        b=CHUNKS[c][0]; h=H[c]
        o=b+core*h
        if lvl>=1: o=o+co[DIMS[c][0]]*(h//4)
        if lvl>=2: o=o+co[DIMS[c][1]]*(h//16)
        return al(o)
    for c in range(3):
        for x in st3[c]: x.wait()
        n=H[c]//16; s=pl.ds(off(c,2),n)
        a_ref[s,:]=(p2[c][0]+p2[c][1])+(p2[c][2]+p2[c][3])
        st4.append([send(a_ref.at[s],a_ref.at[s],peer(DIMS[c][1],d)) for d in range(1,4)])
    st5=[]
    for c in range(3):
        for x in st4[c]: x.wait()
        s=pl.ds(off(c,1),H[c]//4)
        st5.append([send(a_ref.at[s],a_ref.at[s],peer(DIMS[c][0],d)) for d in range(1,4)])
    st6=[]
    for c in range(3):
        for x in st5[c]: x.wait()
        s=pl.ds(off(c,0),H[c])
        st6.append(send(a_ref.at[s],a_ref.at[s],partner))
    for x in st6: x.wait()
def comm_call(g):
    H=[n//2 for _,n in CHUNKS]
    V=lambda *s: pltpu.VMEM(s,F32)
    scr=[V(h,128) for h in H]+[V(3,h//4,128) for h in H]+[V(3,h//16,128) for h in H]+[V(h,128) for h in H]+[V(h//4,128) for h in H]+[V(4,h//16,128) for h in H]
    return pl.pallas_call(comm_kernel,out_shape=jax.ShapeDtypeStruct((ROWS,128),F32),
        in_specs=[pl.BlockSpec(memory_space=pltpu.VMEM)],out_specs=pl.BlockSpec(memory_space=pltpu.VMEM),
        scratch_shapes=scr+[pltpu.SemaphoreType.DMA((60,)),pltpu.SemaphoreType.DMA((60,))],
        compiler_params=pltpu.CompilerParams(collective_id=0,has_side_effects=True,vmem_limit_bytes=40*2**20))(g)
from jax.sharding import PartitionSpec as P
def local(readings,values,counts,prior_root,prior_info):
    g=gram_call(counts,prior_info,readings,values,prior_root)
    a=comm_call(g)
    R,y=chol_call(a,a[INFO:INFO+8])
    rows=lax.dynamic_slice_in_dim(R,lax.axis_index("blk")*64,64,0)
    return rows,y.reshape(1024)
def solution(mesh):
    placed=(P(("fibre","blk"),None),P(("fibre","blk")),P(("fibre","blk")),P(("fibre","blk"),None),P(("fibre","blk")))
    return jax.shard_map(local,mesh=mesh,in_specs=placed,out_specs=(P("blk",None),P()),check_vma=False)
```

```python
import jax, jax.numpy as jnp, numpy as np
from jax import lax
from jax.experimental import pallas as pl
from jax.experimental.pallas import tpu as pltpu
F32=jnp.float32
def bc(x,shape): return jnp.broadcast_to(x,shape)

def factor_block(T, n=16, W=256):
    out=[]
    sub=lax.broadcasted_iota(jnp.int32,(8,128),0)
    for p in range(n):
        V=T[p]
        C=[bc(V[:,8*p+c:8*p+c+1],(8,128)) for c in range(8)]
        Q={q:[bc(T[q][:,8*p+c:8*p+c+1],(8,128)) for c in range(8)] for q in range(p+1,n)}
        Vp=[V[:,128*w:128*w+128] for w in range(W//128)]
        rv=jnp.zeros((8,128),F32)
        rs=[];
        LQ={q:[] for q in Q}
        rows=[]
        for j in range(8):
            d=bc(C[j][j:j+1,:],(8,128))
            r=lax.rsqrt(d)
            L=C[j]*r
            Lm=jnp.where(sub>j,L,0.0) if j<7 else None
            rv=jnp.where(sub==j,r,rv)
            Rj=[bc(v[j:j+1,:],(8,128))*r for v in Vp]
            rows.append(Rj)
            if j<7:
                Vp=[v-Lm*rj for v,rj in zip(Vp,Rj)]
                Ls={k:bc(L[k:k+1,:],(8,128)) for k in range(j+1,8)}
                for k in range(j+1,8): C[k]=C[k]-L*Ls[k]
            for q in Q:
                Lq=Q[q][j]*r
                LQ[q].append(Lq)
                if j<7:
                    for k in range(j+1,8): Q[q][k]=Q[q][k]-Lq*Ls[k]
        out.append(jnp.concatenate([v*rv for v in Vp],axis=1))
        for q in Q:
            parts=[T[q][:,128*w:128*w+128] for w in range(W//128)]
            for j in range(8):
                parts=[a-LQ[q][j]*rj for a,rj in zip(parts,rows[j])]
            T[q]=jnp.concatenate(parts,axis=1)
    return out
def row(x,j): return bc(x[j:j+1,:],(8,128))
def col(x,j): return bc(x[:,j:j+1],(8,128))
def factor_inplace(T,slide=True):
    T=list(T)
    sub=lax.broadcasted_iota(jnp.int32,(8,128),0); lane=lax.broadcasted_iota(jnp.int32,(8,128),1)
    R=[];I=[]
    C=[col(T[0],c) for c in range(8)]
    for p in range(16):
        lo=8*p
        inpan=(lane>=lo)&(lane<lo+8)
        VA=T[p]
        VX=jnp.where(inpan,jnp.where(lane==sub+lo,1.0,0.0),T[p])
        Q={q:[col(T[q],lo+c) for c in range(8)] for q in range(p+1,16)}
        Cn=[col(T[p+1],lo+8+c) for c in range(8)] if p<15 and slide else None
        LQ={q:[] for q in Q}; RX=[]
        oA=jnp.zeros((8,128),F32); oX=jnp.zeros((8,128),F32)
        for j in (0,2,4,6):
            a=row(C[j],j); b=row(C[j],j+1); c=row(C[j+1],j+1)
            det=a*c-b*b
            r1=lax.rsqrt(a); rd=lax.rsqrt(det); r2=r1*rd
            W=a*C[j+1]-b*C[j]
            s1=r1*r1; s2=r2*r2
            L1=C[j]*r1; L2=W*r2
            c1={k:row(C[j],k) for k in range(j+1,8)}
            w2={k:row(W,k) for k in range(j+2,8)}
            l1={k:c1[k]*r1 for k in c1}; l2={k:w2[k]*r2 for k in w2}
            for k in range(j+2,8):
                if k<j+4: C[k]=(C[k]-(C[j]*c1[k])*s1)-(W*w2[k])*s2
                else: C[k]=(C[k]-L1*l1[k])-L2*l2[k]
            g=a*r2
            res=[]
            for V in (VA,VX):
                v0=row(V,j); v1=row(V,j+1)
                res.append((v0*r1,(a*v1-b*v0)*r2))
            (A0,A1),(X0,X1)=res
            RX+= [X0,X1]
            oA=jnp.where(sub==j,A0,jnp.where(sub==j+1,A1,oA))
            oX=jnp.where(sub==j,X0,jnp.where(sub==j+1,X1,oX))
            if j<6:
                L1m=jnp.where(sub>j+1,L1,0.0); L2m=jnp.where(sub>j+1,L2,0.0)
                VA=VA-L1m*A0-L2m*A1
                VX=VX-L1m*X0-L2m*X1
            for q in Q:
                q0=Q[q][j]*r1
                q1=(Q[q][j+1]-q0*l1[j+1])*g
                LQ[q]+=[q0,q1]
                for k in range(j+2,8): Q[q][k]=Q[q][k]-q0*l1[k]-q1*l2[k]
        R.append(jnp.where(lane<lo+8,oA,oX)); I.append(oX)
        if p<15:
            for q in Q:
                t=jnp.where(inpan,0.0,T[q])
                for j in range(8): t=t-LQ[q][j]*RX[j]
                T[q]=t
            if slide:
                for k in range(8):
                    t=Cn[k]
                    for j in range(8): t=t-LQ[p+1][j]*row(LQ[p+1][j],k)
                    Cn[k]=t
                C=Cn
            else: C=[col(T[p+1],lo+8+c) for c in range(8)]
    return R,I
BF=jnp.bfloat16
def split3(x):
    h=x.astype(BF).astype(F32); r=x-h; m=r.astype(BF).astype(F32); l=r-m
    return h,m,l
def outer6(x):
    h,m,l=split3(x)
    a=jnp.concatenate([h,h,m,m,h,l],axis=0)
    b=jnp.concatenate([h,m,h,m,l,h],axis=0).astype(BF)
    return jnp.dot(a.T.astype(BF),b,preferred_element_type=F32)
def factor_inplace2(T,G=3,order="mxu"):
    T=list(T)
    sub=lax.broadcasted_iota(jnp.int32,(8,128),0); lane=lax.broadcasted_iota(jnp.int32,(8,128),1)
    R=[];I=[]
    C=[col(T[0],c) for c in range(8)]
    for p in range(16):
        lo=8*p
        inpan=(lane>=lo)&(lane<lo+8)
        VA=T[p]
        VX=jnp.where(inpan,jnp.where(lane==sub+lo,1.0,0.0),T[p])
        near=range(p+1,min(p+1+G,16)); far=range(p+1+G,16)
        Q={q:[col(T[q],lo+c) for c in range(8)] for q in near}
        Cn=[col(T[p+1],lo+8+c) for c in range(8)] if p<15 else None
        LQ={q:[] for q in near}; RX=[]
        oA=jnp.zeros((8,128),F32); oX=jnp.zeros((8,128),F32)
        for j in (0,2,4,6):
            a=row(C[j],j); b=row(C[j],j+1); c=row(C[j+1],j+1)
            det=a*c-b*b
            r1=lax.rsqrt(a); rd=lax.rsqrt(det); r2=r1*rd
            W=a*C[j+1]-b*C[j]
            s1=r1*r1; s2=r2*r2
            L1=C[j]*r1; L2=W*r2
            c1={k:row(C[j],k) for k in range(j+1,8)}
            w2={k:row(W,k) for k in range(j+2,8)}
            l1={k:c1[k]*r1 for k in c1}; l2={k:w2[k]*r2 for k in w2}
            for k in range(j+2,8):
                if k<j+4: C[k]=(C[k]-(C[j]*c1[k])*s1)-(W*w2[k])*s2
                else: C[k]=(C[k]-L1*l1[k])-L2*l2[k]
            g=a*r2
            res=[]
            for V in (VA,VX):
                v0=row(V,j); v1=row(V,j+1)
                res.append((v0*r1,(a*v1-b*v0)*r2))
            (A0,A1),(X0,X1)=res
            RX+= [X0,X1]
            oA=jnp.where(sub==j,A0,jnp.where(sub==j+1,A1,oA))
            oX=jnp.where(sub==j,X0,jnp.where(sub==j+1,X1,oX))
            if j<6:
                L1m=jnp.where(sub>j+1,L1,0.0); L2m=jnp.where(sub>j+1,L2,0.0)
                VA=VA-L1m*A0-L2m*A1
                VX=VX-L1m*X0-L2m*X1
            for q in Q:
                q0=Q[q][j]*r1
                q1=(Q[q][j+1]-q0*l1[j+1])*g
                LQ[q]+=[q0,q1]
                for k in range(j+2,8): Q[q][k]=Q[q][k]-q0*l1[k]-q1*l2[k]
        R.append(jnp.where(lane<lo+8,oA,oX)); I.append(oX)
        if p<15:
            if len(far):
                D=outer6(oX)
            for q in near:
                t=jnp.where(inpan,0.0,T[q])
                for j in range(8): t=t-LQ[q][j]*RX[j]
                T[q]=t
            for k in range(8):
                t=Cn[k]
                for j in range(8): t=t-LQ[p+1][j]*row(LQ[p+1][j],k)
                Cn[k]=t
            C=Cn
            for q in far:
                T[q]=jnp.where(inpan,0.0,T[q])-D[8*q:8*q+8,:]
    return R,I
def split3b(x):
    h=x.astype(BF); r=x-h.astype(F32); m=r.astype(BF); l=(r-m.astype(F32)).astype(BF)
    return h,m,l
def lhs6(x):
    h,m,l=split3b(x); return jnp.concatenate([h,h,m,m,h,l],axis=1)
def rhs6(x):
    h,m,l=split3b(x); return jnp.concatenate([h,m,h,m,l,h],axis=0)
def bidx(k,j): return 8*k-k*(k-1)//2+(j-k)
def blk(k,j): return pl.ds(brow(bidx(k,j)),128)
def chol_kernel(a_ref,r_ref,y_ref,A,Rs,Li):
    ii=lax.broadcasted_iota(jnp.int32,(8,128),0); jj=lax.broadcasted_iota(jnp.int32,(8,128),1)
    big=(128,128)
    eye=lax.broadcasted_iota(jnp.int32,big,0)==lax.broadcasted_iota(jnp.int32,big,1)
    dg=[jnp.sum(jnp.where(eye,a_ref[blk(k,k),:],0.0),axis=0,keepdims=True) for k in range(8)]
    dr=[lax.rsqrt(d) for d in dg]
    for k in range(8):
        dc=bc(dr[k],big).T
        for j in range(k,8): A[blk(k,j),:]=a_ref[blk(k,j),:]*dc*dr[j]
    bl=[a_ref[INFO+k:INFO+k+1,:]*dr[k] for k in range(8)]
    for k in range(8):
        o=brow(bidx(k,k))
        R,I=factor_inplace2([A[o+8*p:o+8*p+8,:] for p in range(16)])
        for p in range(16):
            Rs[128*k+8*p:128*k+8*p+8,128*k:128*k+128]=jnp.where(jj>=ii+8*p,R[p],0.0)
            Li[8*p:8*p+8,:]=jnp.where(jj<8*p+8,I[p],0.0)
        if k: Rs[128*k:128*k+128,:128*k]=jnp.zeros((128,128*k),F32)
        Linv=Li[...]
        bk=jnp.concatenate([bl[k],jnp.zeros((7,128),F32)],axis=0)
        yk=lax.dot_general(bk,Linv,(((1,),(1,)),((),())),precision=lax.Precision.HIGHEST,preferred_element_type=F32)
        y_ref[k:k+1,:]=yk[0:1,:]
        n=7-k
        if n==0: break
        row_=jnp.concatenate([A[blk(k,j),:] for j in range(k+1,8)],axis=1)
        Rk=jnp.dot(lhs6(Linv),rhs6(row_),preferred_element_type=F32)
        Rs[128*k:128*k+128,128*(k+1):]=Rk
        X=jnp.concatenate([lhs6(Rk[:,128*i:128*i+128].T) for i in range(n)]+[lhs6(jnp.concatenate([yk,jnp.zeros((8,128),F32)],axis=0))],axis=0)
        Y=rhs6(Rk)
        for c in range(0,n,2):
            w=min(2,n-c)
            rows=128*(c+w)
            D=jnp.dot(jnp.concatenate([X[128*n:],X[:rows]],axis=0),Y[:,128*c:128*(c+w)],preferred_element_type=F32)
            for u in range(w):
                j=k+1+c+u
                bl[j]=bl[j]-D[0:1,128*u:128*u+128]
                for i in range(k+1,j+1):
                    z=16+128*(i-k-1)
                    A[blk(i,j),:]=A[blk(i,j),:]-D[z:z+128,128*u:128*u+128]
    s=pl.multiple_of(rowstart(),64)
    for j in range(8):
        r_ref[:,128*j:128*j+128]=Rs[pl.ds(s,64),128*j:128*j+128]*(dg[j]*dr[j])
def rowstart(): return lax.axis_index("blk")*64
def chol_call(a):
    return pl.pallas_call(chol_kernel,out_shape=(jax.ShapeDtypeStruct((64,1024),F32),jax.ShapeDtypeStruct((8,128),F32)),
      in_specs=[pl.BlockSpec(memory_space=pltpu.VMEM)],
      scratch_shapes=[pltpu.VMEM((ROWS,128),F32),pltpu.VMEM((1024,1024),F32),pltpu.VMEM((128,128),F32)],compiler_params=pltpu.CompilerParams(vmem_limit_bytes=32*2**20))(a)
NS=1024; CAP=4096
CH=1024
def brow(i): return 128*i if i<12 else 128*i+256
INFO=1536
ROWS=4864
def gram_kernel(cnt_ref,pi_ref,x_ref,v_ref,pr_ref,g_ref):
    s=pl.program_id(0)
    x=x_ref[...]
    rowi=lax.broadcasted_iota(jnp.int32,(CH,NS),0)+s*CH
    xm=jnp.where(rowi<cnt_ref[0],x,jnp.zeros((),BF))
    xt=x.T
    vf=v_ref[pl.ds(pl.multiple_of(s*(CH//128),8),CH//128),:].astype(F32)
    v=jnp.broadcast_to(jnp.concatenate([vf[i:i+1,:] for i in range(CH//128)],axis=1),(16,CH)).astype(BF)
    def accum(first,xt,v,xm):
        lhs=jnp.concatenate([v,xt],axis=0)
        for c in range(4):
            D=lax.dot_general(lhs[:16+256*(c+1)],xm[:,256*c:256*c+256],(((1,),(0,)),((),())),preferred_element_type=F32)
            for u in range(2):
                j=2*c+u
                dv=D[0:1,128*u:128*u+128]
                if first: g_ref[INFO+j:INFO+j+1,:]=dv
                else: g_ref[INFO+j:INFO+j+1,:]=g_ref[INFO+j:INFO+j+1,:]+dv
                for i in range(j+1):
                    z=16+128*i; o=brow(bidx(i,j))
                    if first: g_ref[o:o+128,:]=D[z:z+128,128*u:128*u+128]
                    else: g_ref[o:o+128,:]=g_ref[o:o+128,:]+D[z:z+128,128*u:128*u+128]
    @pl.when(s==0)
    def _():
        accum(True,xt,v,xm)
        g_ref[INFO+8:INFO+256,:]=jnp.zeros((248,128),F32)
    @pl.when(s>0)
    def _(): accum(False,xt,v,xm)
    @pl.when(s==pl.num_programs(0)-1)
    def _():
        sub=lax.broadcasted_iota(jnp.int32,(8,128),0)
        pv=jnp.zeros((8,128),F32)
        for i in range(8): pv=jnp.where(sub==i,pi_ref[i],pv)
        pr=jnp.concatenate([pr_ref[...],pv],axis=1)
        h,m,l=split3b(pr)
        h,m,l=[t.astype(F32) for t in (h,m,l)]
        z=jnp.zeros((80,NS+128),F32)
        a=jnp.concatenate([h,h,m,m,h,l,z],axis=0)
        b=jnp.concatenate([h,m,h,m,l,h,z],axis=0)[:,:NS].astype(BF)
        at=a.T.astype(BF)
        accum(False,at[:NS],at[NS:NS+16],b)
def gram_call(counts,prior_info,readings,values,prior_root):
    return pl.pallas_call(gram_kernel,grid=(CAP//CH,),
        in_specs=[pl.BlockSpec(memory_space=pltpu.SMEM),pl.BlockSpec(memory_space=pltpu.SMEM),
                  pl.BlockSpec((CH,NS),lambda s:(s,0)),pl.BlockSpec((CAP//128,128),lambda s:(0,0)),
                  pl.BlockSpec((8,NS),lambda s:(0,0))],
        out_specs=pl.BlockSpec(memory_space=pltpu.VMEM),
        out_shape=jax.ShapeDtypeStruct((ROWS,128),F32),
        compiler_params=pltpu.CompilerParams(vmem_limit_bytes=56*2**20))(counts,prior_info,readings,values.reshape(CAP//128,128),prior_root)
MESH=pl.DeviceIdType.MESH
CHUNKS=((0,1792),(1792,1536),(3328,1536))
DIMS=((0,1,2),(1,2,0),(2,0,1))
def comm_kernel(g_ref,a_ref,*scr):
    (r0,r1,r2,p0,p1,p2,ssem,rsem)=(scr[0:3],scr[3:6],scr[6:9],scr[9:12],scr[12:15],scr[15:18],scr[18],scr[19])
    f=lax.axis_index("fibre"); q=lax.axis_index("blk")
    core=f%2; co=(q//4,q%4,f//2)
    def peer(dim,d):
        c=list(co); c[dim]=(c[dim]+d)%4
        return (c[2]*2+core,c[0]*4+c[1])
    partner=(co[2]*2+(1-core),q)
    bar=pltpu.get_barrier_semaphore()
    pl.semaphore_signal(bar,inc=1,device_id=partner,device_id_type=MESH)
    for dim in range(3):
        for d in range(1,4):
            pl.semaphore_signal(bar,inc=1,device_id=peer(dim,d),device_id_type=MESH)
    pl.semaphore_wait(bar,10)
    cnt=[0]
    def send(src,dst,dev):
        i=cnt[0]; cnt[0]+=1
        c=pltpu.make_async_remote_copy(src_ref=src,dst_ref=dst,send_sem=ssem.at[i],recv_sem=rsem.at[i],device_id=dev,device_id_type=MESH)
        c.start(); return c
    al=lambda v: pl.multiple_of(v,8)
    H=[n//2 for _,n in CHUNKS]
    cs=[]
    for c,(b,n) in enumerate(CHUNKS):
        cs.append(send(g_ref.at[pl.ds(al(b+(1-core)*H[c]),H[c])],r0[c],partner))
    st=[]
    for c,(b,n) in enumerate(CHUNKS):
        cs[c].wait()
        p0[c][...]=g_ref[pl.ds(al(b+core*H[c]),H[c]),:]+r0[c][...]
        Q=H[c]//4; dim=DIMS[c][0]
        st.append([send(p0[c].at[pl.ds(al(((co[dim]+d)%4)*Q),Q)],r1[c].at[d-1],peer(dim,d)) for d in range(1,4)])
    st2=[]
    for c in range(3):
        for x in st[c]: x.wait()
        Q=H[c]//4; dim=DIMS[c][0]
        p1[c][...]=(p0[c][pl.ds(al(co[dim]*Q),Q),:]+r1[c][0])+(r1[c][1]+r1[c][2])
        Q2=Q//4; dim=DIMS[c][1]
        st2.append([send(p1[c].at[pl.ds(al(((co[dim]+d)%4)*Q2),Q2)],r2[c].at[d-1],peer(dim,d)) for d in range(1,4)])
    st3=[]
    for c in range(3):
        for x in st2[c]: x.wait()
        Q2=H[c]//16; dim=DIMS[c][1]; dz=DIMS[c][2]
        me=co[dz]
        p2[c][me]=(p1[c][pl.ds(al(co[dim]*Q2),Q2),:]+r2[c][0])+(r2[c][1]+r2[c][2])
        st3.append([send(p2[c].at[me],p2[c].at[me],peer(dz,d)) for d in range(1,4)])
    st4=[]
    def off(c,lvl):
        b=CHUNKS[c][0]; h=H[c]
        o=b+core*h
        if lvl>=1: o=o+co[DIMS[c][0]]*(h//4)
        if lvl>=2: o=o+co[DIMS[c][1]]*(h//16)
        return al(o)
    for c in range(3):
        for x in st3[c]: x.wait()
        n=H[c]//16; s=pl.ds(off(c,2),n)
        a_ref[s,:]=(p2[c][0]+p2[c][1])+(p2[c][2]+p2[c][3])
        st4.append([send(a_ref.at[s],a_ref.at[s],peer(DIMS[c][1],d)) for d in range(1,4)])
    st5=[]
    for c in range(3):
        for x in st4[c]: x.wait()
        s=pl.ds(off(c,1),H[c]//4)
        st5.append([send(a_ref.at[s],a_ref.at[s],peer(DIMS[c][0],d)) for d in range(1,4)])
    st6=[]
    for c in range(3):
        for x in st5[c]: x.wait()
        s=pl.ds(off(c,0),H[c])
        st6.append(send(a_ref.at[s],a_ref.at[s],partner))
    for x in st6: x.wait()
def comm_call(g):
    H=[n//2 for _,n in CHUNKS]
    V=lambda *s: pltpu.VMEM(s,F32)
    scr=[V(h,128) for h in H]+[V(3,h//4,128) for h in H]+[V(3,h//16,128) for h in H]+[V(h,128) for h in H]+[V(h//4,128) for h in H]+[V(4,h//16,128) for h in H]
    return pl.pallas_call(comm_kernel,out_shape=jax.ShapeDtypeStruct((ROWS,128),F32),
        in_specs=[pl.BlockSpec(memory_space=pltpu.VMEM)],out_specs=pl.BlockSpec(memory_space=pltpu.VMEM),
        scratch_shapes=scr+[pltpu.SemaphoreType.DMA((60,)),pltpu.SemaphoreType.DMA((60,))],
        compiler_params=pltpu.CompilerParams(collective_id=0,has_side_effects=True,vmem_limit_bytes=40*2**20))(g)
from jax.sharding import PartitionSpec as P
def local(readings,values,counts,prior_root,prior_info):
    g=gram_call(counts,prior_info,readings,values,prior_root)
    a=comm_call(g)
    rows,y=chol_call(a)
    return rows,y.reshape(1024)
def solution(mesh):
    placed=(P(("fibre","blk"),None),P(("fibre","blk")),P(("fibre","blk")),P(("fibre","blk"),None),P(("fibre","blk")))
    return jax.shard_map(local,mesh=mesh,in_specs=placed,out_specs=(P("blk",None),P()),check_vma=False)
```

```python
import jax, jax.numpy as jnp, numpy as np
from jax import lax
from jax.experimental import pallas as pl
from jax.experimental.pallas import tpu as pltpu
F32=jnp.float32
def bc(x,shape): return jnp.broadcast_to(x,shape)

def factor_block(T, n=16, W=256):
    out=[]
    sub=lax.broadcasted_iota(jnp.int32,(8,128),0)
    for p in range(n):
        V=T[p]
        C=[bc(V[:,8*p+c:8*p+c+1],(8,128)) for c in range(8)]
        Q={q:[bc(T[q][:,8*p+c:8*p+c+1],(8,128)) for c in range(8)] for q in range(p+1,n)}
        Vp=[V[:,128*w:128*w+128] for w in range(W//128)]
        rv=jnp.zeros((8,128),F32)
        rs=[];
        LQ={q:[] for q in Q}
        rows=[]
        for j in range(8):
            d=bc(C[j][j:j+1,:],(8,128))
            r=lax.rsqrt(d)
            L=C[j]*r
            Lm=jnp.where(sub>j,L,0.0) if j<7 else None
            rv=jnp.where(sub==j,r,rv)
            Rj=[bc(v[j:j+1,:],(8,128))*r for v in Vp]
            rows.append(Rj)
            if j<7:
                Vp=[v-Lm*rj for v,rj in zip(Vp,Rj)]
                Ls={k:bc(L[k:k+1,:],(8,128)) for k in range(j+1,8)}
                for k in range(j+1,8): C[k]=C[k]-L*Ls[k]
            for q in Q:
                Lq=Q[q][j]*r
                LQ[q].append(Lq)
                if j<7:
                    for k in range(j+1,8): Q[q][k]=Q[q][k]-Lq*Ls[k]
        out.append(jnp.concatenate([v*rv for v in Vp],axis=1))
        for q in Q:
            parts=[T[q][:,128*w:128*w+128] for w in range(W//128)]
            for j in range(8):
                parts=[a-LQ[q][j]*rj for a,rj in zip(parts,rows[j])]
            T[q]=jnp.concatenate(parts,axis=1)
    return out
def row(x,j): return bc(x[j:j+1,:],(8,128))
def col(x,j): return bc(x[:,j:j+1],(8,128))
def factor_inplace(T,slide=True):
    T=list(T)
    sub=lax.broadcasted_iota(jnp.int32,(8,128),0); lane=lax.broadcasted_iota(jnp.int32,(8,128),1)
    R=[];I=[]
    C=[col(T[0],c) for c in range(8)]
    for p in range(16):
        lo=8*p
        inpan=(lane>=lo)&(lane<lo+8)
        VA=T[p]
        VX=jnp.where(inpan,jnp.where(lane==sub+lo,1.0,0.0),T[p])
        Q={q:[col(T[q],lo+c) for c in range(8)] for q in range(p+1,16)}
        Cn=[col(T[p+1],lo+8+c) for c in range(8)] if p<15 and slide else None
        LQ={q:[] for q in Q}; RX=[]
        oA=jnp.zeros((8,128),F32); oX=jnp.zeros((8,128),F32)
        for j in (0,2,4,6):
            a=row(C[j],j); b=row(C[j],j+1); c=row(C[j+1],j+1)
            det=a*c-b*b
            r1=lax.rsqrt(a); rd=lax.rsqrt(det); r2=r1*rd
            W=a*C[j+1]-b*C[j]
            s1=r1*r1; s2=r2*r2
            L1=C[j]*r1; L2=W*r2
            c1={k:row(C[j],k) for k in range(j+1,8)}
            w2={k:row(W,k) for k in range(j+2,8)}
            l1={k:c1[k]*r1 for k in c1}; l2={k:w2[k]*r2 for k in w2}
            for k in range(j+2,8):
                if k<j+4: C[k]=(C[k]-(C[j]*c1[k])*s1)-(W*w2[k])*s2
                else: C[k]=(C[k]-L1*l1[k])-L2*l2[k]
            g=a*r2
            res=[]
            for V in (VA,VX):
                v0=row(V,j); v1=row(V,j+1)
                res.append((v0*r1,(a*v1-b*v0)*r2))
            (A0,A1),(X0,X1)=res
            RX+= [X0,X1]
            oA=jnp.where(sub==j,A0,jnp.where(sub==j+1,A1,oA))
            oX=jnp.where(sub==j,X0,jnp.where(sub==j+1,X1,oX))
            if j<6:
                L1m=jnp.where(sub>j+1,L1,0.0); L2m=jnp.where(sub>j+1,L2,0.0)
                VA=VA-L1m*A0-L2m*A1
                VX=VX-L1m*X0-L2m*X1
            for q in Q:
                q0=Q[q][j]*r1
                q1=(Q[q][j+1]-q0*l1[j+1])*g
                LQ[q]+=[q0,q1]
                for k in range(j+2,8): Q[q][k]=Q[q][k]-q0*l1[k]-q1*l2[k]
        R.append(jnp.where(lane<lo+8,oA,oX)); I.append(oX)
        if p<15:
            for q in Q:
                t=jnp.where(inpan,0.0,T[q])
                for j in range(8): t=t-LQ[q][j]*RX[j]
                T[q]=t
            if slide:
                for k in range(8):
                    t=Cn[k]
                    for j in range(8): t=t-LQ[p+1][j]*row(LQ[p+1][j],k)
                    Cn[k]=t
                C=Cn
            else: C=[col(T[p+1],lo+8+c) for c in range(8)]
    return R,I
BF=jnp.bfloat16
def split3(x):
    h=x.astype(BF).astype(F32); r=x-h; m=r.astype(BF).astype(F32); l=r-m
    return h,m,l
def outer6(x):
    h,m,l=split3(x)
    a=jnp.concatenate([h,h,m,m,h,l],axis=0)
    b=jnp.concatenate([h,m,h,m,l,h],axis=0).astype(BF)
    return jnp.dot(a.T.astype(BF),b,preferred_element_type=F32)
def factor_inplace2(T,G=3,order="mxu"):
    T=list(T)
    sub=lax.broadcasted_iota(jnp.int32,(8,128),0); lane=lax.broadcasted_iota(jnp.int32,(8,128),1)
    R=[];I=[]
    C=[col(T[0],c) for c in range(8)]
    for p in range(16):
        lo=8*p
        inpan=(lane>=lo)&(lane<lo+8)
        VA=T[p]
        VX=jnp.where(inpan,jnp.where(lane==sub+lo,1.0,0.0),T[p])
        near=range(p+1,min(p+1+G,16)); far=range(p+1+G,16)
        Q={q:[col(T[q],lo+c) for c in range(8)] for q in near}
        Cn=[col(T[p+1],lo+8+c) for c in range(8)] if p<15 else None
        LQ={q:[] for q in near}; RX=[]
        oA=jnp.zeros((8,128),F32); oX=jnp.zeros((8,128),F32)
        for j in (0,2,4,6):
            a=row(C[j],j); b=row(C[j],j+1); c=row(C[j+1],j+1)
            det=a*c-b*b
            r1=lax.rsqrt(a); rd=lax.rsqrt(det); r2=r1*rd
            W=a*C[j+1]-b*C[j]
            s1=r1*r1; s2=r2*r2
            L1=C[j]*r1; L2=W*r2
            c1={k:row(C[j],k) for k in range(j+1,8)}
            w2={k:row(W,k) for k in range(j+2,8)}
            l1={k:c1[k]*r1 for k in c1}; l2={k:w2[k]*r2 for k in w2}
            for k in range(j+2,8):
                if k<j+4: C[k]=(C[k]-(C[j]*c1[k])*s1)-(W*w2[k])*s2
                else: C[k]=(C[k]-L1*l1[k])-L2*l2[k]
            g=a*r2
            res=[]
            for V in (VA,VX):
                v0=row(V,j); v1=row(V,j+1)
                res.append((v0*r1,(a*v1-b*v0)*r2))
            (A0,A1),(X0,X1)=res
            RX+= [X0,X1]
            oA=jnp.where(sub==j,A0,jnp.where(sub==j+1,A1,oA))
            oX=jnp.where(sub==j,X0,jnp.where(sub==j+1,X1,oX))
            if j<6:
                L1m=jnp.where(sub>j+1,L1,0.0); L2m=jnp.where(sub>j+1,L2,0.0)
                VA=VA-L1m*A0-L2m*A1
                VX=VX-L1m*X0-L2m*X1
            for q in Q:
                q0=Q[q][j]*r1
                q1=(Q[q][j+1]-q0*l1[j+1])*g
                LQ[q]+=[q0,q1]
                for k in range(j+2,8): Q[q][k]=Q[q][k]-q0*l1[k]-q1*l2[k]
        R.append(jnp.where(lane<lo+8,oA,oX)); I.append(oX)
        if p<15:
            if len(far):
                D=outer6(oX)
            for q in near:
                t=jnp.where(inpan,0.0,T[q])
                for j in range(8): t=t-LQ[q][j]*RX[j]
                T[q]=t
            for k in range(8):
                t=Cn[k]
                for j in range(8): t=t-LQ[p+1][j]*row(LQ[p+1][j],k)
                Cn[k]=t
            C=Cn
            for q in far:
                T[q]=jnp.where(inpan,0.0,T[q])-D[8*q:8*q+8,:]
    return R,I
MESH=pl.DeviceIdType.MESH
NS=1024; CAP=4096; CH=1024; STEPS=CAP//CH; ROWS=4608
PIECES=((0,512,(0,1,2)),(512,512,(1,2,0)),(1024,512,(2,0,1)),(1536,1024,(0,1,2)),(2560,1024,(1,2,0)),(3584,1024,(2,0,1)))
HALF=[n//2 for _,n,_ in PIECES]
def split3b(x):
    h=x.astype(BF); r=x-h.astype(F32); m=r.astype(BF); l=(r-m.astype(F32)).astype(BF)
    return h,m,l
def lhs6(x):
    h,m,l=split3b(x); return jnp.concatenate([h,h,m,m,h,l],axis=1)
def rhs6(x):
    h,m,l=split3b(x); return jnp.concatenate([h,m,h,m,l,h],axis=0)
def brow(k,j): return 128*(8*k-k*(k-1)//2+(j-k))
def blk(k,j): return pl.ds(brow(k,j),128)

def gram_part(s,cnt_ref,pi_ref,x_ref,v_ref,pr_ref,g,info):
    x=x_ref[...]
    rowi=lax.broadcasted_iota(jnp.int32,(CH,NS),0)+s*CH
    xm=jnp.where(rowi<cnt_ref[0],x,jnp.zeros((),BF))
    xt=x.T
    vf=v_ref[pl.ds(pl.multiple_of(s*(CH//128),8),CH//128),:].astype(F32)
    v=jnp.broadcast_to(jnp.concatenate([vf[i:i+1,:] for i in range(CH//128)],axis=1),(16,CH)).astype(BF)
    def accum(first,xt,v,xm):
        lhs=jnp.concatenate([v,xt],axis=0)
        for c in range(4):
            D=jnp.dot(lhs[:16+256*(c+1)],xm[:,256*c:256*c+256],preferred_element_type=F32)
            for u in range(2):
                j=2*c+u
                dv=D[0:1,128*u:128*u+128]
                info[j:j+1,:]=dv if first else info[j:j+1,:]+dv
                for i in range(j+1):
                    z=16+128*i; d=D[z:z+128,128*u:128*u+128]
                    g[blk(i,j),:]=d if first else g[blk(i,j),:]+d
    @pl.when(s==0)
    def _(): accum(True,xt,v,xm)
    @pl.when(s>0)
    def _(): accum(False,xt,v,xm)
    @pl.when(s==STEPS-1)
    def _():
        sub=lax.broadcasted_iota(jnp.int32,(8,128),0)
        pv=jnp.zeros((8,128),F32)
        for i in range(8): pv=jnp.where(sub==i,pi_ref[i],pv)
        h,m,l=split3(jnp.concatenate([pr_ref[...],pv],axis=1))
        z=jnp.zeros((80,NS+128),F32)
        a=jnp.concatenate([h,h,m,m,h,l,z],axis=0)
        b=jnp.concatenate([h,m,h,m,l,h,z],axis=0)[:,:NS].astype(BF)
        at=a.T.astype(BF)
        accum(False,at[:NS],at[NS:NS+16],b)
        eye=lax.broadcasted_iota(jnp.int32,(128,128),0)==lax.broadcasted_iota(jnp.int32,(128,128),1)
        lane=lax.broadcasted_iota(jnp.int32,(1,128),1)
        for k in range(8):
            dg=jnp.sum(jnp.where(eye,g[blk(k,k),:],0.0),axis=0,keepdims=True)
            for base,r in ((64,info[k:k+1,:]),(80,dg)):
                rr=pltpu.roll(jnp.broadcast_to(r,(8,128)),64,1)[0:1,:]
                g[base+2*k:base+2*k+1,:]=jnp.where(lane<64,r,g[base+2*k:base+2*k+1,:])
                g[base+2*k+1:base+2*k+2,:]=jnp.where(lane<64,rr,g[base+2*k+1:base+2*k+2,:])

class Comm:
    def __init__(self,g,a,r0,r1,r2,p0,p1,p2,ssem,rsem):
        self.__dict__.update(g=g,a=a,r0=r0,r1=r1,r2=r2,p0=p0,p1=p1,p2=p2,ssem=ssem,rsem=rsem)
        f=lax.axis_index("fibre"); q=lax.axis_index("blk")
        self.core=f%2; self.co=(q//4,q%4,f//2); self.q=q; self.n=0; self.fly={}
        self.partner=(self.co[2]*2+(1-self.core),q)
    def peer(self,dim,d):
        c=list(self.co); c[dim]=(c[dim]+d)%4
        return (c[2]*2+self.core,c[0]*4+c[1])
    def greet(self):
        bar=pltpu.get_barrier_semaphore()
        pl.semaphore_signal(bar,inc=1,device_id=self.partner,device_id_type=MESH)
        for dim in range(3):
            for d in range(1,4):
                pl.semaphore_signal(bar,inc=1,device_id=self.peer(dim,d),device_id_type=MESH)
    def met(self): pl.semaphore_wait(pltpu.get_barrier_semaphore(),10)
    def send(self,src,dst,dev):
        i=self.n; self.n+=1
        c=pltpu.make_async_remote_copy(src_ref=src,dst_ref=dst,send_sem=self.ssem.at[i],recv_sem=self.rsem.at[i],device_id=dev,device_id_type=MESH)
        c.start(); return c
    def off(self,c,lvl):
        b,_,dims=PIECES[c]; h=HALF[c]
        o=b+self.core*h
        if lvl>=1: o=o+self.co[dims[0]]*(h//4)
        if lvl>=2: o=o+self.co[dims[1]]*(h//16)
        return pl.multiple_of(o,8)
    def step(self,n,cs):
        al=lambda v: pl.multiple_of(v,8)
        for c in cs:
            b,_,dims=PIECES[c]; h=HALF[c]; h4=h//4; h16=h//16
            for x in self.fly.pop(c,()): x.wait()
            core,co=self.core,self.co
            if n==0:
                out=[self.send(self.g.at[pl.ds(al(b+(1-core)*h),h)],self.r0[c],self.partner)]
            elif n==1:
                self.p0[c][...]=self.g[pl.ds(al(b+core*h),h),:]+self.r0[c][...]
                out=[self.send(self.p0[c].at[pl.ds(al(((co[dims[0]]+d)%4)*h4),h4)],self.r1[c].at[d-1],self.peer(dims[0],d)) for d in (2,1,3)]
            elif n==2:
                r=self.r1[c]
                self.p1[c][...]=(self.p0[c][pl.ds(al(co[dims[0]]*h4),h4),:]+r[0])+(r[1]+r[2])
                out=[self.send(self.p1[c].at[pl.ds(al(((co[dims[1]]+d)%4)*h16),h16)],self.r2[c].at[d-1],self.peer(dims[1],d)) for d in (2,1,3)]
            elif n==3:
                r=self.r2[c]; me=co[dims[2]]
                self.p2[c][me]=(self.p1[c][pl.ds(al(co[dims[1]]*h16),h16),:]+r[0])+(r[1]+r[2])
                out=[self.send(self.p2[c].at[me],self.p2[c].at[me],self.peer(dims[2],d)) for d in (2,1,3)]
            elif n==4:
                s=pl.ds(self.off(c,2),h16); t=self.p2[c]
                self.a[s,:]=(t[0]+t[1])+(t[2]+t[3])
                out=[self.send(self.a.at[s],self.a.at[s],self.peer(dims[1],d)) for d in (2,1,3)]
            elif n==5:
                s=pl.ds(self.off(c,1),h4)
                out=[self.send(self.a.at[s],self.a.at[s],self.peer(dims[0],d)) for d in (2,1,3)]
            elif n==6:
                s=pl.ds(self.off(c,0),h)
                out=[self.send(self.a.at[s],self.a.at[s],self.partner)]
            else: out=[]
            self.fly[c]=out

def body(cnt_ref,pi_ref,x_ref,v_ref,pr_ref,o_ref,y_ref,g,info,a,A,Rs,Li,Xs,Ys,*scr):
    s=pl.program_id(0)
    k6=lambda i: scr[6*i:6*i+6]
    cm=Comm(g,a,k6(0),k6(1),k6(2),k6(3),k6(4),k6(5),scr[36],scr[37])
    @pl.when(s==0)
    def _(): cm.greet()
    gram_part(s,cnt_ref,pi_ref,x_ref,v_ref,pr_ref,g,info)
    @pl.when(s==STEPS-1)
    def _(): rest(cm,o_ref,y_ref,a,A,Rs,Li,Xs,Ys)

def rest(cm,o_ref,y_ref,a,A,Rs,Li,Xs,Ys):
    P0=(0,1,2); P1=(3,4,5)
    cm.met()
    for n,cs in ((0,P0),(0,P1),(1,P0),(1,P1),(2,P0),(3,P0),(2,P1),(4,P0),(3,P1),(5,P0),(4,P1),(6,P0),(5,P1),(7,P0)): cm.step(n,cs)
    ii=lax.broadcasted_iota(jnp.int32,(8,128),0); jj=lax.broadcasted_iota(jnp.int32,(8,128),1)
    big=(128,128)
    l16=lax.broadcasted_iota(jnp.int32,(16,128),1)
    def unpack(base):
        e=a[base:base+16,:]; er=pltpu.roll(e,64,1)
        return [jnp.where(l16[:1]<64,e[2*k:2*k+1,:],er[2*k+1:2*k+2,:]) for k in range(8)]
    dg=unpack(80); dr=[lax.rsqrt(d) for d in dg]
    bl=[b*d for b,d in zip(unpack(64),dr)]
    a00=a[0:128,:]
    low=(lax.broadcasted_iota(jnp.int32,big,0)>=64)&(lax.broadcasted_iota(jnp.int32,big,1)<64)
    dc=[bc(d,big).T for d in dr]
    A[0:128,:]=jnp.where(low,a00.T,a00)*dc[0]*dr[0]
    def scale(k,j): A[blk(k,j),:]=a[blk(k,j),:]*dc[k]*dr[j]
    for j in range(1,8): scale(0,j)
    for j in range(1,5): scale(1,j)
    def factor(k):
        o=brow(k,k)
        R,I=factor_inplace2([A[o+8*p:o+8*p+8,:] for p in range(16)])
        for p in range(16):
            Rs[128*k+8*p:128*k+8*p+8,128*k:128*k+128]=jnp.where(jj>=ii+8*p,R[p],0.0)
            Li[8*p:8*p+8,:]=jnp.where(jj<8*p+8,I[p],0.0)
        if k: Rs[128*k:128*k+128,:128*k]=jnp.zeros((128,128*k),F32)
    def panel(k):
        Linv=Li[...]
        bk=jnp.concatenate([bl[k],jnp.zeros((7,128),F32)],axis=0)
        yk=lax.dot_general(bk,Linv,(((1,),(1,)),((),())),precision=lax.Precision.HIGHEST,preferred_element_type=F32)
        y_ref[k:k+1,:]=yk[0:1,:]
        n=7-k
        if n==0: return
        row_=jnp.concatenate([A[blk(k,j),:] for j in range(k+1,8)],axis=1)
        Rk=jnp.dot(lhs6(Linv),rhs6(row_),preferred_element_type=F32)
        Rs[128*k:128*k+128,128*(k+1):]=Rk
        Xs[0:16,:]=lhs6(jnp.concatenate([yk,jnp.zeros((8,128),F32)],axis=0))
        for i in range(n): Xs[16+128*i:144+128*i,:]=lhs6(Rk[:,128*i:128*i+128].T)
        Ys[:,:128*n]=rhs6(Rk)
    def update(k,j0,j1,i0,i1,withb):
        lo=0 if withb else 16+128*(i0-k-1)
        if withb and i0>k+1: X=jnp.concatenate([Xs[0:16,:],Xs[16+128*(i0-k-1):16+128*(i1-k-1),:]],axis=0)
        else: X=Xs[lo:16+128*(i1-k-1),:]
        D=jnp.dot(X,Ys[:,128*(j0-k-1):128*(j1-k-1)],preferred_element_type=F32)
        b0=16 if withb else 0
        for j in range(j0,j1):
            u=128*(j-j0)
            if withb: bl[j]=bl[j]-D[0:1,u:u+128]
            for i in range(i0,min(i1,j+1)):
                z=b0+128*(i-i0)
                A[blk(i,j),:]=A[blk(i,j),:]-D[z:z+128,u:u+128]
    factor(0)
    cm.step(6,P1)
    panel(0)
    update(0,1,5,1,2,True)
    factor(1)
    cm.step(7,P1)
    for k in range(1,8):
        for j in range(max(k,5) if k==1 else k,8): scale(k,j)
    update(0,5,8,1,8,True)
    update(0,2,3,2,3,False)
    update(0,3,5,2,5,False)
    for k in range(1,8):
        panel(k)
        if k==7: break
        for j in range(k+1,8,2): update(k,j,min(j+2,8),k+1,min(j+2,8),True)
        factor(k+1)
    s=pl.multiple_of(cm.q*64,64)
    for j in range(8):
        o_ref[:,128*j:128*j+128]=Rs[pl.ds(s,64),128*j:128*j+128]*(dg[j]*dr[j])

def local(readings,values,counts,prior_root,prior_info):
    V=lambda *s: pltpu.VMEM(s,F32)
    H=HALF
    scr=[V(ROWS,128),V(8,128),V(ROWS,128),V(ROWS,128),V(NS,NS),V(128,128),pltpu.VMEM((16+7*128,768),BF),pltpu.VMEM((768,896),BF)]
    scr+=[V(h,128) for h in H]+[V(3,h//4,128) for h in H]+[V(3,h//16,128) for h in H]+[V(h,128) for h in H]+[V(h//4,128) for h in H]+[V(4,h//16,128) for h in H]
    scr+=[pltpu.SemaphoreType.DMA((102,)),pltpu.SemaphoreType.DMA((102,))]
    smem=pl.BlockSpec(memory_space=pltpu.SMEM)
    root,y=pl.pallas_call(body,grid=(STEPS,),
        in_specs=[smem,smem,pl.BlockSpec((CH,NS),lambda s:(s,0)),pl.BlockSpec((CAP//128,128),lambda s:(0,0)),pl.BlockSpec((8,NS),lambda s:(0,0))],
        out_specs=(pl.BlockSpec((64,NS),lambda s:(0,0)),pl.BlockSpec((8,128),lambda s:(0,0))),
        out_shape=(jax.ShapeDtypeStruct((64,NS),F32),jax.ShapeDtypeStruct((8,128),F32)),
        scratch_shapes=scr,
        compiler_params=pltpu.CompilerParams(collective_id=0,has_side_effects=True,vmem_limit_bytes=58*2**20),
    )(counts,prior_info,readings,values.reshape(CAP//128,128),prior_root)
    return root,y.reshape(NS)
from jax.sharding import PartitionSpec as P
def solution(mesh):
    placed=(P(("fibre","blk"),None),P(("fibre","blk")),P(("fibre","blk")),P(("fibre","blk"),None),P(("fibre","blk")))
    return jax.shard_map(local,mesh=mesh,in_specs=placed,out_specs=(P("blk",None),P()),check_vma=False)
```

```python
import jax, jax.numpy as jnp, numpy as np
from jax import lax
from jax.experimental import pallas as pl
from jax.experimental.pallas import tpu as pltpu
F32=jnp.float32
def bc(x,shape): return jnp.broadcast_to(x,shape)

def factor_block(T, n=16, W=256):
    out=[]
    sub=lax.broadcasted_iota(jnp.int32,(8,128),0)
    for p in range(n):
        V=T[p]
        C=[bc(V[:,8*p+c:8*p+c+1],(8,128)) for c in range(8)]
        Q={q:[bc(T[q][:,8*p+c:8*p+c+1],(8,128)) for c in range(8)] for q in range(p+1,n)}
        Vp=[V[:,128*w:128*w+128] for w in range(W//128)]
        rv=jnp.zeros((8,128),F32)
        rs=[];
        LQ={q:[] for q in Q}
        rows=[]
        for j in range(8):
            d=bc(C[j][j:j+1,:],(8,128))
            r=lax.rsqrt(d)
            L=C[j]*r
            Lm=jnp.where(sub>j,L,0.0) if j<7 else None
            rv=jnp.where(sub==j,r,rv)
            Rj=[bc(v[j:j+1,:],(8,128))*r for v in Vp]
            rows.append(Rj)
            if j<7:
                Vp=[v-Lm*rj for v,rj in zip(Vp,Rj)]
                Ls={k:bc(L[k:k+1,:],(8,128)) for k in range(j+1,8)}
                for k in range(j+1,8): C[k]=C[k]-L*Ls[k]
            for q in Q:
                Lq=Q[q][j]*r
                LQ[q].append(Lq)
                if j<7:
                    for k in range(j+1,8): Q[q][k]=Q[q][k]-Lq*Ls[k]
        out.append(jnp.concatenate([v*rv for v in Vp],axis=1))
        for q in Q:
            parts=[T[q][:,128*w:128*w+128] for w in range(W//128)]
            for j in range(8):
                parts=[a-LQ[q][j]*rj for a,rj in zip(parts,rows[j])]
            T[q]=jnp.concatenate(parts,axis=1)
    return out
def row(x,j): return bc(x[j:j+1,:],(8,128))
def col(x,j): return bc(x[:,j:j+1],(8,128))
def factor_inplace(T,slide=True):
    T=list(T)
    sub=lax.broadcasted_iota(jnp.int32,(8,128),0); lane=lax.broadcasted_iota(jnp.int32,(8,128),1)
    R=[];I=[]
    C=[col(T[0],c) for c in range(8)]
    for p in range(16):
        lo=8*p
        inpan=(lane>=lo)&(lane<lo+8)
        VA=T[p]
        VX=jnp.where(inpan,jnp.where(lane==sub+lo,1.0,0.0),T[p])
        Q={q:[col(T[q],lo+c) for c in range(8)] for q in range(p+1,16)}
        Cn=[col(T[p+1],lo+8+c) for c in range(8)] if p<15 and slide else None
        LQ={q:[] for q in Q}; RX=[]
        oA=jnp.zeros((8,128),F32); oX=jnp.zeros((8,128),F32)
        for j in (0,2,4,6):
            a=row(C[j],j); b=row(C[j],j+1); c=row(C[j+1],j+1)
            det=a*c-b*b
            r1=lax.rsqrt(a); rd=lax.rsqrt(det); r2=r1*rd
            W=a*C[j+1]-b*C[j]
            s1=r1*r1; s2=r2*r2
            L1=C[j]*r1; L2=W*r2
            c1={k:row(C[j],k) for k in range(j+1,8)}
            w2={k:row(W,k) for k in range(j+2,8)}
            l1={k:c1[k]*r1 for k in c1}; l2={k:w2[k]*r2 for k in w2}
            for k in range(j+2,8):
                if k<j+4: C[k]=(C[k]-(C[j]*c1[k])*s1)-(W*w2[k])*s2
                else: C[k]=(C[k]-L1*l1[k])-L2*l2[k]
            g=a*r2
            res=[]
            for V in (VA,VX):
                v0=row(V,j); v1=row(V,j+1)
                res.append((v0*r1,(a*v1-b*v0)*r2))
            (A0,A1),(X0,X1)=res
            RX+= [X0,X1]
            oA=jnp.where(sub==j,A0,jnp.where(sub==j+1,A1,oA))
            oX=jnp.where(sub==j,X0,jnp.where(sub==j+1,X1,oX))
            if j<6:
                L1m=jnp.where(sub>j+1,L1,0.0); L2m=jnp.where(sub>j+1,L2,0.0)
                VA=VA-L1m*A0-L2m*A1
                VX=VX-L1m*X0-L2m*X1
            for q in Q:
                q0=Q[q][j]*r1
                q1=(Q[q][j+1]-q0*l1[j+1])*g
                LQ[q]+=[q0,q1]
                for k in range(j+2,8): Q[q][k]=Q[q][k]-q0*l1[k]-q1*l2[k]
        R.append(jnp.where(lane<lo+8,oA,oX)); I.append(oX)
        if p<15:
            for q in Q:
                t=jnp.where(inpan,0.0,T[q])
                for j in range(8): t=t-LQ[q][j]*RX[j]
                T[q]=t
            if slide:
                for k in range(8):
                    t=Cn[k]
                    for j in range(8): t=t-LQ[p+1][j]*row(LQ[p+1][j],k)
                    Cn[k]=t
                C=Cn
            else: C=[col(T[p+1],lo+8+c) for c in range(8)]
    return R,I
BF=jnp.bfloat16
def split3(x):
    h=x.astype(BF).astype(F32); r=x-h; m=r.astype(BF).astype(F32); l=r-m
    return h,m,l
def outer6(xs,lo,lane):
    n=len(xs)
    x=jnp.concatenate(xs,axis=0)
    z=jnp.concatenate([t if i==n-1 else jnp.where((lane>=lo-8*(n-2-i))&(lane<lo+8),0.0,t) for i,t in enumerate(xs)],axis=0)
    h,m,l=split3(x); zh,zm,zl=split3(z)
    a=jnp.concatenate([h,h,m,m,h,l],axis=0)
    b=jnp.concatenate([zh,zm,zh,zm,zl,zh],axis=0).astype(BF)
    return jnp.dot(a.T.astype(BF),b,preferred_element_type=F32)
def factor_inplace2(T,G=3,B=2):
    T=list(T)
    sub=lax.broadcasted_iota(jnp.int32,(8,128),0); lane=lax.broadcasted_iota(jnp.int32,(8,128),1)
    R=[];I=[]
    C=[col(T[0],c) for c in range(8)]
    for p in range(16):
        lo=8*p
        inpan=(lane>=lo)&(lane<lo+8); inbat=(lane>=lo-8*(p%B))&(lane<lo+8)
        VA=T[p]
        VX=jnp.where(inpan,jnp.where(lane==sub+lo,1.0,0.0),T[p])
        end=min(p-p%B+B+G,16); near=range(p+1,end); far=range(end,16) if p%B==B-1 else ()
        Q={q:[col(T[q],lo+c) for c in range(8)] for q in near}
        Cn=[col(T[p+1],lo+8+c) for c in range(8)] if p<15 else None
        LQ={q:[] for q in near}; RX=[]
        oA=jnp.zeros((8,128),F32); oX=jnp.zeros((8,128),F32)
        for j in (0,2,4,6):
            a=row(C[j],j); b=row(C[j],j+1); c=row(C[j+1],j+1)
            det=a*c-b*b
            r1=lax.rsqrt(a); rd=lax.rsqrt(det); r2=r1*rd
            W=a*C[j+1]-b*C[j]
            s1=r1*r1; s2=r2*r2
            L1=C[j]*r1; L2=W*r2
            c1={k:row(C[j],k) for k in range(j+1,8)}
            w2={k:row(W,k) for k in range(j+2,8)}
            l1={k:c1[k]*r1 for k in c1}; l2={k:w2[k]*r2 for k in w2}
            for k in range(j+2,8):
                if k<j+4: C[k]=(C[k]-(C[j]*c1[k])*s1)-(W*w2[k])*s2
                else: C[k]=(C[k]-L1*l1[k])-L2*l2[k]
            g=a*r2
            res=[]
            for V in (VA,VX):
                v0=row(V,j); v1=row(V,j+1)
                res.append((v0*r1,(a*v1-b*v0)*r2))
            (A0,A1),(X0,X1)=res
            RX+= [X0,X1]
            oA=jnp.where(sub==j,A0,jnp.where(sub==j+1,A1,oA))
            oX=jnp.where(sub==j,X0,jnp.where(sub==j+1,X1,oX))
            if j<6:
                L1m=jnp.where(sub>j+1,L1,0.0); L2m=jnp.where(sub>j+1,L2,0.0)
                VA=VA-L1m*A0-L2m*A1
                VX=VX-L1m*X0-L2m*X1
            for q in Q:
                q0=Q[q][j]*r1
                q1=(Q[q][j+1]-q0*l1[j+1])*g
                LQ[q]+=[q0,q1]
                for k in range(j+2,8): Q[q][k]=Q[q][k]-q0*l1[k]-q1*l2[k]
        R.append(jnp.where(lane<lo+8,oA,oX)); I.append(oX)
        if p<15:
            if len(far):
                D=outer6(I[-B:],lo,lane)
            for q in near:
                t=jnp.where(inpan,0.0,T[q])
                for j in range(8): t=t-LQ[q][j]*RX[j]
                T[q]=t
            for k in range(8):
                t=Cn[k]
                for j in range(8): t=t-LQ[p+1][j]*row(LQ[p+1][j],k)
                Cn[k]=t
            C=Cn
            for q in far:
                T[q]=jnp.where(inbat,0.0,T[q])-D[8*q:8*q+8,:]
    return R,I
MESH=pl.DeviceIdType.MESH
NS=1024; CAP=4096; ROWS=4608; SLABS=(512,512,1024,1024,1024)
PIECES=((0,512,(0,1,2)),(512,512,(1,2,0)),(1024,512,(2,0,1)),(1536,1024,(0,1,2)),(2560,1024,(1,2,0)),(3584,1024,(2,0,1)))
HALF=[n//2 for _,n,_ in PIECES]
def split3b(x):
    h=x.astype(BF); r=x-h.astype(F32); m=r.astype(BF); l=(r-m.astype(F32)).astype(BF)
    return h,m,l
def lhs6(x):
    h,m,l=split3b(x); return jnp.concatenate([h,h,m,m,h,l],axis=1)
def rhs6(x):
    h,m,l=split3b(x); return jnp.concatenate([h,m,h,m,l,h],axis=0)
def brow(k,j): return 128*(8*k-k*(k-1)//2+(j-k))
def blk(k,j): return pl.ds(brow(k,j),128)

def gram_part(cnt_ref,pi_ref,x_hbm,v_ref,pr_ref,g,info,xb,xsem):
    cps=[]; at=0
    for i,n in enumerate(SLABS):
        cp=pltpu.make_async_copy(x_hbm.at[pl.ds(at,n)],xb.at[pl.ds(at,n)],xsem.at[i]); cp.start()
        cps.append((cp,at,n)); at+=n
    def accum(first,lhs,rhs,v):
        Dv=jnp.dot(v,rhs,preferred_element_type=F32)
        for j in range(8):
            dv=Dv[0:1,128*j:128*j+128]
            info[j:j+1,:]=dv if first else info[j:j+1,:]+dv
        for c in range(4):
            D=lax.dot_general(lhs[:,:256*(c+1)],rhs[:,256*c:256*c+256],(((0,),(0,)),((),())),preferred_element_type=F32)
            for u in range(2):
                j=2*c+u
                for i in range(j+1):
                    d=D[128*i:128*i+128,128*u:128*u+128]
                    g[blk(i,j),:]=d if first else g[blk(i,j),:]+d
    sub=lax.broadcasted_iota(jnp.int32,(8,128),0)
    pv=jnp.zeros((8,128),F32)
    for i in range(8): pv=jnp.where(sub==i,pi_ref[i],pv)
    h,m,l=split3(jnp.concatenate([pr_ref[...],pv],axis=1))
    z=jnp.zeros((80,NS+128),F32)
    pa=jnp.concatenate([h,h,m,m,h,l,z],axis=0)
    pb=jnp.concatenate([h,m,h,m,l,h,z],axis=0)[:,:NS].astype(BF)
    accum(True,pa[:,:NS].astype(BF),pb,pa[:,NS:].T[:16].astype(BF))
    for cp,at,n in cps:
        cp.wait()
        x=xb[pl.ds(at,n),:]
        xm=jnp.where(lax.broadcasted_iota(jnp.int32,(n,NS),0)+at<cnt_ref[0],x,jnp.zeros((),BF))
        vf=v_ref[at//128:(at+n)//128,:].astype(F32)
        v=jnp.broadcast_to(jnp.concatenate([vf[i:i+1,:] for i in range(n//128)],axis=1),(16,n)).astype(BF)
        accum(False,x,xm,v)
    eye=lax.broadcasted_iota(jnp.int32,(128,128),0)==lax.broadcasted_iota(jnp.int32,(128,128),1)
    lane=lax.broadcasted_iota(jnp.int32,(1,128),1)
    for k in range(8):
        dg=jnp.sum(jnp.where(eye,g[blk(k,k),:],0.0),axis=0,keepdims=True)
        for base,r in ((64,info[k:k+1,:]),(80,dg)):
            rr=pltpu.roll(jnp.broadcast_to(r,(8,128)),64,1)[0:1,:]
            g[base+2*k:base+2*k+1,:]=jnp.where(lane<64,r,g[base+2*k:base+2*k+1,:])
            g[base+2*k+1:base+2*k+2,:]=jnp.where(lane<64,rr,g[base+2*k+1:base+2*k+2,:])

class Comm:
    def __init__(self,g,a,r0,r1,r2,p0,p1,p2,ssem,rsem):
        self.__dict__.update(g=g,a=a,r0=r0,r1=r1,r2=r2,p0=p0,p1=p1,p2=p2,ssem=ssem,rsem=rsem)
        f=lax.axis_index("fibre"); q=lax.axis_index("blk")
        self.core=f%2; self.co=(q//4,q%4,f//2); self.q=q; self.n=0; self.fly={}
        self.partner=(self.co[2]*2+(1-self.core),q)
    def peer(self,dim,d):
        c=list(self.co); c[dim]=(c[dim]+d)%4
        return (c[2]*2+self.core,c[0]*4+c[1])
    def greet(self):
        bar=pltpu.get_barrier_semaphore()
        pl.semaphore_signal(bar,inc=1,device_id=self.partner,device_id_type=MESH)
        for dim in range(3):
            for d in range(1,4):
                pl.semaphore_signal(bar,inc=1,device_id=self.peer(dim,d),device_id_type=MESH)
    def met(self): pl.semaphore_wait(pltpu.get_barrier_semaphore(),10)
    def send(self,src,dst,dev):
        i=self.n; self.n+=1
        c=pltpu.make_async_remote_copy(src_ref=src,dst_ref=dst,send_sem=self.ssem.at[i],recv_sem=self.rsem.at[i],device_id=dev,device_id_type=MESH)
        c.start(); return c
    def off(self,c,lvl):
        b,_,dims=PIECES[c]; h=HALF[c]
        o=b+self.core*h
        if lvl>=1: o=o+self.co[dims[0]]*(h//4)
        if lvl>=2: o=o+self.co[dims[1]]*(h//16)
        return pl.multiple_of(o,8)
    def step(self,n,cs):
        al=lambda v: pl.multiple_of(v,8)
        for c in cs:
            b,_,dims=PIECES[c]; h=HALF[c]; h4=h//4; h16=h//16
            for x in self.fly.pop(c,()): x.wait()
            core,co=self.core,self.co
            if n==0:
                out=[self.send(self.g.at[pl.ds(al(b+(1-core)*h),h)],self.r0[c],self.partner)]
            elif n==1:
                self.p0[c][...]=self.g[pl.ds(al(b+core*h),h),:]+self.r0[c][...]
                out=[self.send(self.p0[c].at[pl.ds(al(((co[dims[0]]+d)%4)*h4),h4)],self.r1[c].at[d-1],self.peer(dims[0],d)) for d in (2,1,3)]
            elif n==2:
                r=self.r1[c]
                self.p1[c][...]=(self.p0[c][pl.ds(al(co[dims[0]]*h4),h4),:]+r[0])+(r[1]+r[2])
                out=[self.send(self.p1[c].at[pl.ds(al(((co[dims[1]]+d)%4)*h16),h16)],self.r2[c].at[d-1],self.peer(dims[1],d)) for d in (2,1,3)]
            elif n==3:
                r=self.r2[c]; me=co[dims[2]]
                self.p2[c][me]=(self.p1[c][pl.ds(al(co[dims[1]]*h16),h16),:]+r[0])+(r[1]+r[2])
                out=[self.send(self.p2[c].at[me],self.p2[c].at[me],self.peer(dims[2],d)) for d in (2,1,3)]
            elif n==4:
                s=pl.ds(self.off(c,2),h16); t=self.p2[c]
                self.a[s,:]=(t[0]+t[1])+(t[2]+t[3])
                out=[self.send(self.a.at[s],self.a.at[s],self.peer(dims[1],d)) for d in (2,1,3)]
            elif n==5:
                s=pl.ds(self.off(c,1),h4)
                out=[self.send(self.a.at[s],self.a.at[s],self.peer(dims[0],d)) for d in (2,1,3)]
            elif n==6:
                s=pl.ds(self.off(c,0),h)
                out=[self.send(self.a.at[s],self.a.at[s],self.partner)]
            else: out=[]
            self.fly[c]=out

def body(cnt_ref,pi_ref,x_hbm,v_ref,pr_ref,o_ref,y_ref,xb,xsem,g,info,a,A,Rs,Li,Xs,Ys,*scr):
    k6=lambda i: scr[6*i:6*i+6]
    cm=Comm(g,a,k6(0),k6(1),k6(2),k6(3),k6(4),k6(5),scr[36],scr[37])
    cm.greet()
    gram_part(cnt_ref,pi_ref,x_hbm,v_ref,pr_ref,g,info,xb,xsem)
    rest(cm,o_ref,y_ref,a,A,Rs,Li,Xs,Ys)

def rest(cm,o_ref,y_ref,a,A,Rs,Li,Xs,Ys):
    P0=(0,1,2); P1=(3,4,5)
    cm.met()
    for n,cs in ((0,P0),(0,P1),(1,P0),(1,P1),(2,P0),(3,P0),(2,P1),(4,P0),(3,P1),(5,P0),(4,P1),(6,P0),(5,P1),(7,P0)): cm.step(n,cs)
    ii=lax.broadcasted_iota(jnp.int32,(8,128),0); jj=lax.broadcasted_iota(jnp.int32,(8,128),1)
    big=(128,128)
    l16=lax.broadcasted_iota(jnp.int32,(16,128),1)
    def unpack(base):
        e=a[base:base+16,:]; er=pltpu.roll(e,64,1)
        return [jnp.where(l16[:1]<64,e[2*k:2*k+1,:],er[2*k+1:2*k+2,:]) for k in range(8)]
    dg=unpack(80); dr=[lax.rsqrt(d) for d in dg]
    bl=[b*d for b,d in zip(unpack(64),dr)]
    a00=a[0:128,:]
    low=(lax.broadcasted_iota(jnp.int32,big,0)>=64)&(lax.broadcasted_iota(jnp.int32,big,1)<64)
    dc=[bc(d,big).T for d in dr]
    A[0:128,:]=jnp.where(low,a00.T,a00)*dc[0]*dr[0]
    def scale(k,j): A[blk(k,j),:]=a[blk(k,j),:]*dc[k]*dr[j]
    for j in range(1,8): scale(0,j)
    for j in range(1,5): scale(1,j)
    def factor(k):
        o=brow(k,k)
        R,I=factor_inplace2(G=1,B=5,T=[A[o+8*p:o+8*p+8,:] for p in range(16)])
        for p in range(16):
            Rs[128*k+8*p:128*k+8*p+8,128*k:128*k+128]=jnp.where(jj>=ii+8*p,R[p],0.0)
            Li[8*p:8*p+8,:]=jnp.where(jj<8*p+8,I[p],0.0)
        if k: Rs[128*k:128*k+128,:128*k]=jnp.zeros((128,128*k),F32)
    def panel(k):
        Linv=Li[...]
        bk=jnp.concatenate([bl[k],jnp.zeros((7,128),F32)],axis=0)
        yk=lax.dot_general(bk,Linv,(((1,),(1,)),((),())),precision=lax.Precision.HIGHEST,preferred_element_type=F32)
        y_ref[k:k+1,:]=yk[0:1,:]
        n=7-k
        if n==0: return
        row_=jnp.concatenate([A[blk(k,j),:] for j in range(k+1,8)],axis=1)
        Rk=jnp.dot(lhs6(Linv),rhs6(row_),preferred_element_type=F32)
        Rs[128*k:128*k+128,128*(k+1):]=Rk
        Xs[0:16,:]=lhs6(jnp.concatenate([yk,jnp.zeros((8,128),F32)],axis=0))
        for i in range(n): Xs[16+128*i:144+128*i,:]=lhs6(Rk[:,128*i:128*i+128].T)
        Ys[:,:128*n]=rhs6(Rk)
    def update(k,j0,j1,i0,i1,withb):
        lo=0 if withb else 16+128*(i0-k-1)
        if withb and i0>k+1: X=jnp.concatenate([Xs[0:16,:],Xs[16+128*(i0-k-1):16+128*(i1-k-1),:]],axis=0)
        else: X=Xs[lo:16+128*(i1-k-1),:]
        D=jnp.dot(X,Ys[:,128*(j0-k-1):128*(j1-k-1)],preferred_element_type=F32)
        b0=16 if withb else 0
        for j in range(j0,j1):
            u=128*(j-j0)
            if withb: bl[j]=bl[j]-D[0:1,u:u+128]
            for i in range(i0,min(i1,j+1)):
                z=b0+128*(i-i0)
                A[blk(i,j),:]=A[blk(i,j),:]-D[z:z+128,u:u+128]
    factor(0)
    cm.step(6,P1)
    panel(0)
    update(0,1,5,1,2,True)
    factor(1)
    cm.step(7,P1)
    for k in range(1,8):
        for j in range(max(k,5) if k==1 else k,8): scale(k,j)
    update(0,5,8,1,8,True)
    update(0,2,3,2,3,False)
    update(0,3,5,2,5,False)
    for k in range(1,8):
        panel(k)
        if k==7: break
        for j in range(k+1,8,2): update(k,j,min(j+2,8),k+1,min(j+2,8),True)
        factor(k+1)
    s=pl.multiple_of(cm.q*64,64)
    for j in range(8):
        o_ref[:,128*j:128*j+128]=Rs[pl.ds(s,64),128*j:128*j+128]*(dg[j]*dr[j])

def finish(o_in,y_in,o_ref,y_ref):
    o_ref[...]=o_in[...]
    y_ref[...]=y_in[...]

def local(readings,values,counts,prior_root,prior_info):
    V=lambda *s: pltpu.VMEM(s,F32)
    H=HALF
    scr=[pltpu.VMEM((CAP,NS),BF),pltpu.SemaphoreType.DMA((len(SLABS),))]
    scr+=[V(ROWS,128),V(8,128),V(ROWS,128),V(ROWS,128),V(NS,NS),V(128,128),pltpu.VMEM((16+7*128,768),BF),pltpu.VMEM((768,896),BF)]
    scr+=[V(h,128) for h in H]+[V(3,h//4,128) for h in H]+[V(3,h//16,128) for h in H]+[V(h,128) for h in H]+[V(h//4,128) for h in H]+[V(4,h//16,128) for h in H]
    scr+=[pltpu.SemaphoreType.DMA((102,)),pltpu.SemaphoreType.DMA((102,))]
    smem=pl.BlockSpec(memory_space=pltpu.SMEM); vmem=pl.BlockSpec(memory_space=pltpu.VMEM)
    outs=(jax.ShapeDtypeStruct((64,NS),F32),jax.ShapeDtypeStruct((8,128),F32))
    root,y=pl.pallas_call(body,
        in_specs=[smem,smem,pl.BlockSpec(memory_space=pl.ANY),vmem,vmem],
        out_specs=(vmem,vmem),out_shape=outs,scratch_shapes=scr,
        compiler_params=pltpu.CompilerParams(collective_id=0,has_side_effects=True,vmem_limit_bytes=58*2**20),
    )(counts,prior_info,readings,values.reshape(CAP//128,128),prior_root)
    root,y=pl.pallas_call(finish,in_specs=[vmem,vmem],out_specs=(vmem,vmem),out_shape=outs)(root,y)
    return root,y.reshape(NS)
from jax.sharding import PartitionSpec as P
def solution(mesh):
    placed=(P(("fibre","blk"),None),P(("fibre","blk")),P(("fibre","blk")),P(("fibre","blk"),None),P(("fibre","blk")))
    return jax.shard_map(local,mesh=mesh,in_specs=placed,out_specs=(P("blk",None),P()),check_vma=False)
```

```python
import jax, jax.numpy as jnp, numpy as np
from jax import lax
from jax.experimental import pallas as pl
from jax.experimental.pallas import tpu as pltpu
F32=jnp.float32
def bc(x,shape): return jnp.broadcast_to(x,shape)

def factor_block(T, n=16, W=256):
    out=[]
    sub=lax.broadcasted_iota(jnp.int32,(8,128),0)
    for p in range(n):
        V=T[p]
        C=[bc(V[:,8*p+c:8*p+c+1],(8,128)) for c in range(8)]
        Q={q:[bc(T[q][:,8*p+c:8*p+c+1],(8,128)) for c in range(8)] for q in range(p+1,n)}
        Vp=[V[:,128*w:128*w+128] for w in range(W//128)]
        rv=jnp.zeros((8,128),F32)
        rs=[];
        LQ={q:[] for q in Q}
        rows=[]
        for j in range(8):
            d=bc(C[j][j:j+1,:],(8,128))
            r=lax.rsqrt(d)
            L=C[j]*r
            Lm=jnp.where(sub>j,L,0.0) if j<7 else None
            rv=jnp.where(sub==j,r,rv)
            Rj=[bc(v[j:j+1,:],(8,128))*r for v in Vp]
            rows.append(Rj)
            if j<7:
                Vp=[v-Lm*rj for v,rj in zip(Vp,Rj)]
                Ls={k:bc(L[k:k+1,:],(8,128)) for k in range(j+1,8)}
                for k in range(j+1,8): C[k]=C[k]-L*Ls[k]
            for q in Q:
                Lq=Q[q][j]*r
                LQ[q].append(Lq)
                if j<7:
                    for k in range(j+1,8): Q[q][k]=Q[q][k]-Lq*Ls[k]
        out.append(jnp.concatenate([v*rv for v in Vp],axis=1))
        for q in Q:
            parts=[T[q][:,128*w:128*w+128] for w in range(W//128)]
            for j in range(8):
                parts=[a-LQ[q][j]*rj for a,rj in zip(parts,rows[j])]
            T[q]=jnp.concatenate(parts,axis=1)
    return out
def row(x,j): return bc(x[j:j+1,:],(8,128))
def col(x,j): return bc(x[:,j:j+1],(8,128))
def factor_inplace(T,slide=True):
    T=list(T)
    sub=lax.broadcasted_iota(jnp.int32,(8,128),0); lane=lax.broadcasted_iota(jnp.int32,(8,128),1)
    R=[];I=[]
    C=[col(T[0],c) for c in range(8)]
    for p in range(16):
        lo=8*p
        inpan=(lane>=lo)&(lane<lo+8)
        VA=T[p]
        VX=jnp.where(inpan,jnp.where(lane==sub+lo,1.0,0.0),T[p])
        Q={q:[col(T[q],lo+c) for c in range(8)] for q in range(p+1,16)}
        Cn=[col(T[p+1],lo+8+c) for c in range(8)] if p<15 and slide else None
        LQ={q:[] for q in Q}; RX=[]
        oA=jnp.zeros((8,128),F32); oX=jnp.zeros((8,128),F32)
        for j in (0,2,4,6):
            a=row(C[j],j); b=row(C[j],j+1); c=row(C[j+1],j+1)
            det=a*c-b*b
            r1=lax.rsqrt(a); rd=lax.rsqrt(det); r2=r1*rd
            W=a*C[j+1]-b*C[j]
            s1=r1*r1; s2=r2*r2
            L1=C[j]*r1; L2=W*r2
            c1={k:row(C[j],k) for k in range(j+1,8)}
            w2={k:row(W,k) for k in range(j+2,8)}
            l1={k:c1[k]*r1 for k in c1}; l2={k:w2[k]*r2 for k in w2}
            for k in range(j+2,8):
                if k<j+4: C[k]=(C[k]-(C[j]*c1[k])*s1)-(W*w2[k])*s2
                else: C[k]=(C[k]-L1*l1[k])-L2*l2[k]
            g=a*r2
            res=[]
            for V in (VA,VX):
                v0=row(V,j); v1=row(V,j+1)
                res.append((v0*r1,(a*v1-b*v0)*r2))
            (A0,A1),(X0,X1)=res
            RX+= [X0,X1]
            oA=jnp.where(sub==j,A0,jnp.where(sub==j+1,A1,oA))
            oX=jnp.where(sub==j,X0,jnp.where(sub==j+1,X1,oX))
            if j<6:
                L1m=jnp.where(sub>j+1,L1,0.0); L2m=jnp.where(sub>j+1,L2,0.0)
                VA=VA-L1m*A0-L2m*A1
                VX=VX-L1m*X0-L2m*X1
            for q in Q:
                q0=Q[q][j]*r1
                q1=(Q[q][j+1]-q0*l1[j+1])*g
                LQ[q]+=[q0,q1]
                for k in range(j+2,8): Q[q][k]=Q[q][k]-q0*l1[k]-q1*l2[k]
        R.append(jnp.where(lane<lo+8,oA,oX)); I.append(oX)
        if p<15:
            for q in Q:
                t=jnp.where(inpan,0.0,T[q])
                for j in range(8): t=t-LQ[q][j]*RX[j]
                T[q]=t
            if slide:
                for k in range(8):
                    t=Cn[k]
                    for j in range(8): t=t-LQ[p+1][j]*row(LQ[p+1][j],k)
                    Cn[k]=t
                C=Cn
            else: C=[col(T[p+1],lo+8+c) for c in range(8)]
    return R,I
BF=jnp.bfloat16
def split3(x):
    h=x.astype(BF).astype(F32); r=x-h; m=r.astype(BF).astype(F32); l=r-m
    return h,m,l
def outer6(xs,lo,lane):
    n=len(xs)
    x=jnp.concatenate(xs,axis=0)
    z=jnp.concatenate([t if i==n-1 else jnp.where((lane>=lo-8*(n-2-i))&(lane<lo+8),0.0,t) for i,t in enumerate(xs)],axis=0)
    h,m,l=split3(x); zh,zm,zl=split3(z)
    a=jnp.concatenate([h,h,m,m,h,l],axis=0)
    b=jnp.concatenate([zh,zm,zh,zm,zl,zh],axis=0).astype(BF)
    return jnp.dot(a.T.astype(BF),b,preferred_element_type=F32)
def factor_inplace2(T,G=3,B=2):
    T=list(T)
    sub=lax.broadcasted_iota(jnp.int32,(8,128),0); lane=lax.broadcasted_iota(jnp.int32,(8,128),1)
    R=[];I=[]
    C=[col(T[0],c) for c in range(8)]
    for p in range(16):
        lo=8*p
        inpan=(lane>=lo)&(lane<lo+8); inbat=(lane>=lo-8*(p%B))&(lane<lo+8)
        VA=T[p]
        VX=jnp.where(inpan,jnp.where(lane==sub+lo,1.0,0.0),T[p])
        end=min(p-p%B+B+G,16); near=range(p+1,end); far=range(end,16) if p%B==B-1 else ()
        Q={q:[col(T[q],lo+c) for c in range(8)] for q in near}
        Cn=[col(T[p+1],lo+8+c) for c in range(8)] if p<15 else None
        LQ={q:[] for q in near}; RX=[]
        oA=jnp.zeros((8,128),F32); oX=jnp.zeros((8,128),F32)
        for j in (0,2,4,6):
            a=row(C[j],j); b=row(C[j],j+1); c=row(C[j+1],j+1)
            det=a*c-b*b
            r1=lax.rsqrt(a); rd=lax.rsqrt(det); r2=r1*rd
            W=a*C[j+1]-b*C[j]
            s1=r1*r1; s2=r2*r2
            L1=C[j]*r1; L2=W*r2
            c1={k:row(C[j],k) for k in range(j+1,8)}
            w2={k:row(W,k) for k in range(j+2,8)}
            l1={k:c1[k]*r1 for k in c1}; l2={k:w2[k]*r2 for k in w2}
            for k in range(j+2,8):
                if k<j+4: C[k]=(C[k]-(C[j]*c1[k])*s1)-(W*w2[k])*s2
                else: C[k]=(C[k]-L1*l1[k])-L2*l2[k]
            g=a*r2
            res=[]
            for V in (VA,VX):
                v0=row(V,j); v1=row(V,j+1)
                res.append((v0*r1,(a*v1-b*v0)*r2))
            (A0,A1),(X0,X1)=res
            RX+= [X0,X1]
            oA=jnp.where(sub==j,A0,jnp.where(sub==j+1,A1,oA))
            oX=jnp.where(sub==j,X0,jnp.where(sub==j+1,X1,oX))
            if j<6:
                L1m=jnp.where(sub>j+1,L1,0.0); L2m=jnp.where(sub>j+1,L2,0.0)
                VA=VA-L1m*A0-L2m*A1
                VX=VX-L1m*X0-L2m*X1
            for q in Q:
                q0=Q[q][j]*r1
                q1=(Q[q][j+1]-q0*l1[j+1])*g
                LQ[q]+=[q0,q1]
                for k in range(j+2,8): Q[q][k]=Q[q][k]-q0*l1[k]-q1*l2[k]
        R.append(jnp.where(lane<lo+8,oA,oX)); I.append(oX)
        if p<15:
            if len(far):
                D=outer6(I[-B:],lo,lane)
            for q in near:
                t=jnp.where(inpan,0.0,T[q])
                for j in range(8): t=t-LQ[q][j]*RX[j]
                T[q]=t
            for k in range(8):
                t=Cn[k]
                for j in range(8): t=t-LQ[p+1][j]*row(LQ[p+1][j],k)
                Cn[k]=t
            C=Cn
            for q in far:
                T[q]=jnp.where(inbat,0.0,T[q])-D[8*q:8*q+8,:]
    return R,I
MESH=pl.DeviceIdType.MESH
NS=1024; CAP=4096; ROWS=4608; SLABS=(512,512,1024,1024,1024)
PIECES=((0,512,(0,1,2)),(512,512,(1,2,0)),(1024,512,(2,0,1)),(1536,1024,(0,1,2)),(2560,1024,(1,2,0)),(3584,1024,(2,0,1)))
HALF=[n//2 for _,n,_ in PIECES]
def split3b(x):
    h=x.astype(BF); r=x-h.astype(F32); m=r.astype(BF); l=(r-m.astype(F32)).astype(BF)
    return h,m,l
def lhs6(x):
    h,m,l=split3b(x); return jnp.concatenate([h,h,m,m,h,l],axis=1)
def rhs6(x):
    h,m,l=split3b(x); return jnp.concatenate([h,m,h,m,l,h],axis=0)
def brow(k,j): return 128*(8*k-k*(k-1)//2+(j-k))
def blk(k,j): return pl.ds(brow(k,j),128)

def gram_part(cnt_ref,pi_ref,x_hbm,v_ref,pr_ref,g,info,xb,xsem):
    cps=[]; at=0
    for i,n in enumerate(SLABS):
        cp=pltpu.make_async_copy(x_hbm.at[pl.ds(at,n)],xb.at[pl.ds(at,n)],xsem.at[i]); cp.start()
        cps.append((cp,at,n)); at+=n
    def accum(first,lhs,rhs,v):
        Dv=jnp.dot(v,rhs,preferred_element_type=F32)
        for j in range(8):
            dv=Dv[0:1,128*j:128*j+128]
            info[j:j+1,:]=dv if first else info[j:j+1,:]+dv
        for c in range(4):
            D=lax.dot_general(lhs[:,:256*(c+1)],rhs[:,256*c:256*c+256],(((0,),(0,)),((),())),preferred_element_type=F32)
            for u in range(2):
                j=2*c+u
                for i in range(j+1):
                    d=D[128*i:128*i+128,128*u:128*u+128]
                    g[blk(i,j),:]=d if first else g[blk(i,j),:]+d
    sub=lax.broadcasted_iota(jnp.int32,(8,128),0)
    pv=jnp.zeros((8,128),F32)
    for i in range(8): pv=jnp.where(sub==i,pi_ref[i],pv)
    h,m,l=split3(jnp.concatenate([pr_ref[...],pv],axis=1))
    z=jnp.zeros((80,NS+128),F32)
    pa=jnp.concatenate([h,h,m,m,h,l,z],axis=0)
    pb=jnp.concatenate([h,m,h,m,l,h,z],axis=0)[:,:NS].astype(BF)
    accum(True,pa[:,:NS].astype(BF),pb,pa[:,NS:].T[:16].astype(BF))
    for cp,at,n in cps:
        cp.wait()
        x=xb[pl.ds(at,n),:]
        xm=jnp.where(lax.broadcasted_iota(jnp.int32,(n,NS),0)+at<cnt_ref[0],x,jnp.zeros((),BF))
        vf=v_ref[at//128:(at+n)//128,:].astype(F32)
        v=jnp.broadcast_to(jnp.concatenate([vf[i:i+1,:] for i in range(n//128)],axis=1),(16,n)).astype(BF)
        accum(False,x,xm,v)
    eye=lax.broadcasted_iota(jnp.int32,(128,128),0)==lax.broadcasted_iota(jnp.int32,(128,128),1)
    lane=lax.broadcasted_iota(jnp.int32,(1,128),1)
    for k in range(8):
        dg=jnp.sum(jnp.where(eye,g[blk(k,k),:],0.0),axis=0,keepdims=True)
        for base,r in ((64,info[k:k+1,:]),(80,dg)):
            rr=pltpu.roll(jnp.broadcast_to(r,(8,128)),64,1)[0:1,:]
            g[base+2*k:base+2*k+1,:]=jnp.where(lane<64,r,g[base+2*k:base+2*k+1,:])
            g[base+2*k+1:base+2*k+2,:]=jnp.where(lane<64,rr,g[base+2*k+1:base+2*k+2,:])

class Comm:
    def __init__(self,g,a,r0,r1,r2,p0,p1,p2,ssem,rsem):
        self.__dict__.update(g=g,a=a,r0=r0,r1=r1,r2=r2,p0=p0,p1=p1,p2=p2,ssem=ssem,rsem=rsem)
        f=lax.axis_index("fibre"); q=lax.axis_index("blk")
        self.core=f%2; self.co=(q//4,q%4,f//2); self.q=q; self.n=0; self.fly={}
        self.partner=(self.co[2]*2+(1-self.core),q)
    def peer(self,dim,d):
        c=list(self.co); c[dim]=(c[dim]+d)%4
        return (c[2]*2+self.core,c[0]*4+c[1])
    def greet(self):
        bar=pltpu.get_barrier_semaphore()
        pl.semaphore_signal(bar,inc=1,device_id=self.partner,device_id_type=MESH)
        for dim in range(3):
            for d in range(1,4):
                pl.semaphore_signal(bar,inc=1,device_id=self.peer(dim,d),device_id_type=MESH)
    def met(self): pl.semaphore_wait(pltpu.get_barrier_semaphore(),10)
    def send(self,src,dst,dev):
        i=self.n; self.n+=1
        c=pltpu.make_async_remote_copy(src_ref=src,dst_ref=dst,send_sem=self.ssem.at[i],recv_sem=self.rsem.at[i],device_id=dev,device_id_type=MESH)
        c.start(); return c
    def off(self,c,lvl):
        b,_,dims=PIECES[c]; h=HALF[c]
        o=b+self.core*h
        if lvl>=1: o=o+self.co[dims[0]]*(h//4)
        if lvl>=2: o=o+self.co[dims[1]]*(h//16)
        return pl.multiple_of(o,8)
    def step(self,n,cs):
        al=lambda v: pl.multiple_of(v,8)
        for c in cs:
            b,_,dims=PIECES[c]; h=HALF[c]; h4=h//4; h16=h//16
            if n==5 and c<3: continue
            for x in self.fly.pop(c,()): x.wait()
            core,co=self.core,self.co
            if n==0:
                out=[self.send(self.g.at[pl.ds(al(b+(1-core)*h),h)],self.r0[c],self.partner)]
            elif n==1:
                self.p0[c][...]=self.g[pl.ds(al(b+core*h),h),:]+self.r0[c][...]
                out=[self.send(self.p0[c].at[pl.ds(al(((co[dims[0]]+d)%4)*h4),h4)],self.r1[c].at[d-1],self.peer(dims[0],d)) for d in (2,1,3)]
            elif n==2 and c<3:
                r=self.r1[c]; me=co[dims[1]]
                self.r2[c][me]=(self.p0[c][pl.ds(al(co[dims[0]]*h4),h4),:]+r[0])+(r[1]+r[2])
                out=[self.send(self.r2[c].at[me],self.r2[c].at[me],self.peer(dims[1],d)) for d in (2,1,3)]
            elif n==3 and c<3:
                t=self.r2[c]; me=co[dims[2]]
                self.p2[c][me]=(t[0]+t[1])+(t[2]+t[3])
                out=[self.send(self.p2[c].at[me],self.p2[c].at[me],self.peer(dims[2],d)) for d in (2,1,3)]
            elif n==4 and c<3:
                s=pl.ds(self.off(c,1),h4); t=self.p2[c]
                self.a[s,:]=(t[0]+t[1])+(t[2]+t[3])
                out=[self.send(self.a.at[s],self.a.at[s],self.peer(dims[0],d)) for d in (2,1,3)]
            elif n==2:
                r=self.r1[c]
                self.p1[c][...]=(self.p0[c][pl.ds(al(co[dims[0]]*h4),h4),:]+r[0])+(r[1]+r[2])
                out=[self.send(self.p1[c].at[pl.ds(al(((co[dims[1]]+d)%4)*h16),h16)],self.r2[c].at[d-1],self.peer(dims[1],d)) for d in (2,1,3)]
            elif n==3:
                r=self.r2[c]; me=co[dims[2]]
                self.p2[c][me]=(self.p1[c][pl.ds(al(co[dims[1]]*h16),h16),:]+r[0])+(r[1]+r[2])
                out=[self.send(self.p2[c].at[me],self.p2[c].at[me],self.peer(dims[2],d)) for d in (2,1,3)]
            elif n==4:
                s=pl.ds(self.off(c,2),h16); t=self.p2[c]
                self.a[s,:]=(t[0]+t[1])+(t[2]+t[3])
                out=[self.send(self.a.at[s],self.a.at[s],self.peer(dims[1],d)) for d in (2,1,3)]
            elif n==5:
                s=pl.ds(self.off(c,1),h4)
                out=[self.send(self.a.at[s],self.a.at[s],self.peer(dims[0],d)) for d in (2,1,3)]
            elif n==6:
                s=pl.ds(self.off(c,0),h)
                out=[self.send(self.a.at[s],self.a.at[s],self.partner)]
            else: out=[]
            self.fly[c]=out

def body(cnt_ref,pi_ref,x_hbm,v_ref,pr_ref,o_ref,y_ref,xb,xsem,g,info,a,A,Rs,Li,Xs,Ys,*scr):
    k6=lambda i: scr[6*i:6*i+6]
    cm=Comm(g,a,k6(0),k6(1),k6(2),k6(3),k6(4),k6(5),scr[36],scr[37])
    cm.greet()
    gram_part(cnt_ref,pi_ref,x_hbm,v_ref,pr_ref,g,info,xb,xsem)
    rest(cm,o_ref,y_ref,a,A,Rs,Li,Xs,Ys)

def rest(cm,o_ref,y_ref,a,A,Rs,Li,Xs,Ys):
    P0=(0,1,2); P1=(3,4,5)
    cm.met()
    for n,cs in ((0,P0),(0,P1),(1,P0),(1,P1),(2,P0),(2,P1),(3,P0),(3,P1),(4,P0),(4,P1),(6,P0),(5,P1),(7,P0)): cm.step(n,cs)
    ii=lax.broadcasted_iota(jnp.int32,(8,128),0); jj=lax.broadcasted_iota(jnp.int32,(8,128),1)
    big=(128,128)
    l16=lax.broadcasted_iota(jnp.int32,(16,128),1)
    def unpack(base):
        e=a[base:base+16,:]; er=pltpu.roll(e,64,1)
        return [jnp.where(l16[:1]<64,e[2*k:2*k+1,:],er[2*k+1:2*k+2,:]) for k in range(8)]
    dg=unpack(80); dr=[lax.rsqrt(d) for d in dg]
    bl=[b*d for b,d in zip(unpack(64),dr)]
    a00=a[0:128,:]
    low=(lax.broadcasted_iota(jnp.int32,big,0)>=64)&(lax.broadcasted_iota(jnp.int32,big,1)<64)
    dc=[bc(d,big).T for d in dr]
    A[0:128,:]=jnp.where(low,a00.T,a00)*dc[0]*dr[0]
    def scale(k,j): A[blk(k,j),:]=a[blk(k,j),:]*dc[k]*dr[j]
    for j in range(1,8): scale(0,j)
    for j in range(1,5): scale(1,j)
    def factor(k):
        o=brow(k,k)
        R,I=factor_inplace2(G=1,B=5,T=[A[o+8*p:o+8*p+8,:] for p in range(16)])
        for p in range(16):
            Rs[128*k+8*p:128*k+8*p+8,128*k:128*k+128]=jnp.where(jj>=ii+8*p,R[p],0.0)
            Li[8*p:8*p+8,:]=jnp.where(jj<8*p+8,I[p],0.0)
        if k: Rs[128*k:128*k+128,:128*k]=jnp.zeros((128,128*k),F32)
    def panel(k):
        Linv=Li[...]
        bk=jnp.concatenate([bl[k],jnp.zeros((7,128),F32)],axis=0)
        yk=lax.dot_general(bk,Linv,(((1,),(1,)),((),())),precision=lax.Precision.HIGHEST,preferred_element_type=F32)
        y_ref[k:k+1,:]=yk[0:1,:]
        n=7-k
        if n==0: return
        row_=jnp.concatenate([A[blk(k,j),:] for j in range(k+1,8)],axis=1)
        Rk=jnp.dot(lhs6(Linv),rhs6(row_),preferred_element_type=F32)
        Rs[128*k:128*k+128,128*(k+1):]=Rk
        Xs[0:16,:]=lhs6(jnp.concatenate([yk,jnp.zeros((8,128),F32)],axis=0))
        for i in range(n): Xs[16+128*i:144+128*i,:]=lhs6(Rk[:,128*i:128*i+128].T)
        Ys[:,:128*n]=rhs6(Rk)
    def update(k,j0,j1,i0,i1,withb):
        lo=0 if withb else 16+128*(i0-k-1)
        if withb and i0>k+1: X=jnp.concatenate([Xs[0:16,:],Xs[16+128*(i0-k-1):16+128*(i1-k-1),:]],axis=0)
        else: X=Xs[lo:16+128*(i1-k-1),:]
        D=jnp.dot(X,Ys[:,128*(j0-k-1):128*(j1-k-1)],preferred_element_type=F32)
        b0=16 if withb else 0
        for j in range(j0,j1):
            u=128*(j-j0)
            if withb: bl[j]=bl[j]-D[0:1,u:u+128]
            for i in range(i0,min(i1,j+1)):
                z=b0+128*(i-i0)
                A[blk(i,j),:]=A[blk(i,j),:]-D[z:z+128,u:u+128]
    factor(0)
    cm.step(6,P1)
    panel(0)
    update(0,1,5,1,2,True)
    factor(1)
    cm.step(7,P1)
    for k in range(1,8):
        for j in range(max(k,5) if k==1 else k,8): scale(k,j)
    update(0,5,8,1,8,True)
    update(0,2,3,2,3,False)
    update(0,3,5,2,5,False)
    for k in range(1,8):
        panel(k)
        if k==7: break
        for j in range(k+1,8,2): update(k,j,min(j+2,8),k+1,min(j+2,8),True)
        factor(k+1)
    s=pl.multiple_of(cm.q*64,64)
    for j in range(8):
        o_ref[:,128*j:128*j+128]=Rs[pl.ds(s,64),128*j:128*j+128]*(dg[j]*dr[j])

def finish(o_in,y_in,o_ref,y_ref):
    o_ref[...]=o_in[...]
    y_ref[...]=y_in[...]

def local(readings,values,counts,prior_root,prior_info):
    V=lambda *s: pltpu.VMEM(s,F32)
    H=HALF
    scr=[pltpu.VMEM((CAP,NS),BF),pltpu.SemaphoreType.DMA((len(SLABS),))]
    scr+=[V(ROWS,128),V(8,128),V(ROWS,128),V(ROWS,128),V(NS,NS),V(128,128),pltpu.VMEM((16+7*128,768),BF),pltpu.VMEM((768,896),BF)]
    scr+=[V(h,128) for h in H]+[V(3,h//4,128) for h in H]+[V(4,h//4,128) if i<3 else V(3,h//16,128) for i,h in enumerate(H)]+[V(h,128) for h in H]+[V(h//4,128) for h in H]+[V(4,h//4 if i<3 else h//16,128) for i,h in enumerate(H)]
    scr+=[pltpu.SemaphoreType.DMA((102,)),pltpu.SemaphoreType.DMA((102,))]
    smem=pl.BlockSpec(memory_space=pltpu.SMEM); vmem=pl.BlockSpec(memory_space=pltpu.VMEM)
    outs=(jax.ShapeDtypeStruct((64,NS),F32),jax.ShapeDtypeStruct((8,128),F32))
    root,y=pl.pallas_call(body,
        in_specs=[smem,smem,pl.BlockSpec(memory_space=pl.ANY),vmem,vmem],
        out_specs=(vmem,vmem),out_shape=outs,scratch_shapes=scr,
        compiler_params=pltpu.CompilerParams(collective_id=0,has_side_effects=True,vmem_limit_bytes=58*2**20),
    )(counts,prior_info,readings,values.reshape(CAP//128,128),prior_root)
    root,y=pl.pallas_call(finish,in_specs=[vmem,vmem],out_specs=(vmem,vmem),out_shape=outs)(root,y)
    return root,y.reshape(NS)
from jax.sharding import PartitionSpec as P
def solution(mesh):
    placed=(P(("fibre","blk"),None),P(("fibre","blk")),P(("fibre","blk")),P(("fibre","blk"),None),P(("fibre","blk")))
    return jax.shard_map(local,mesh=mesh,in_specs=placed,out_specs=(P("blk",None),P()),check_vma=False)
```

```python
import jax, jax.numpy as jnp, numpy as np
from jax import lax
from jax.experimental import pallas as pl
from jax.experimental.pallas import tpu as pltpu
F32=jnp.float32
def bc(x,shape): return jnp.broadcast_to(x,shape)

def factor_block(T, n=16, W=256):
    out=[]
    sub=lax.broadcasted_iota(jnp.int32,(8,128),0)
    for p in range(n):
        V=T[p]
        C=[bc(V[:,8*p+c:8*p+c+1],(8,128)) for c in range(8)]
        Q={q:[bc(T[q][:,8*p+c:8*p+c+1],(8,128)) for c in range(8)] for q in range(p+1,n)}
        Vp=[V[:,128*w:128*w+128] for w in range(W//128)]
        rv=jnp.zeros((8,128),F32)
        rs=[];
        LQ={q:[] for q in Q}
        rows=[]
        for j in range(8):
            d=bc(C[j][j:j+1,:],(8,128))
            r=lax.rsqrt(d)
            L=C[j]*r
            Lm=jnp.where(sub>j,L,0.0) if j<7 else None
            rv=jnp.where(sub==j,r,rv)
            Rj=[bc(v[j:j+1,:],(8,128))*r for v in Vp]
            rows.append(Rj)
            if j<7:
                Vp=[v-Lm*rj for v,rj in zip(Vp,Rj)]
                Ls={k:bc(L[k:k+1,:],(8,128)) for k in range(j+1,8)}
                for k in range(j+1,8): C[k]=C[k]-L*Ls[k]
            for q in Q:
                Lq=Q[q][j]*r
                LQ[q].append(Lq)
                if j<7:
                    for k in range(j+1,8): Q[q][k]=Q[q][k]-Lq*Ls[k]
        out.append(jnp.concatenate([v*rv for v in Vp],axis=1))
        for q in Q:
            parts=[T[q][:,128*w:128*w+128] for w in range(W//128)]
            for j in range(8):
                parts=[a-LQ[q][j]*rj for a,rj in zip(parts,rows[j])]
            T[q]=jnp.concatenate(parts,axis=1)
    return out
def row(x,j): return bc(x[j:j+1,:],(8,128))
def col(x,j): return bc(x[:,j:j+1],(8,128))
def factor_inplace(T,slide=True):
    T=list(T)
    sub=lax.broadcasted_iota(jnp.int32,(8,128),0); lane=lax.broadcasted_iota(jnp.int32,(8,128),1)
    R=[];I=[]
    C=[col(T[0],c) for c in range(8)]
    for p in range(16):
        lo=8*p
        inpan=(lane>=lo)&(lane<lo+8)
        VA=T[p]
        VX=jnp.where(inpan,jnp.where(lane==sub+lo,1.0,0.0),T[p])
        Q={q:[col(T[q],lo+c) for c in range(8)] for q in range(p+1,16)}
        Cn=[col(T[p+1],lo+8+c) for c in range(8)] if p<15 and slide else None
        LQ={q:[] for q in Q}; RX=[]
        oA=jnp.zeros((8,128),F32); oX=jnp.zeros((8,128),F32)
        for j in (0,2,4,6):
            a=row(C[j],j); b=row(C[j],j+1); c=row(C[j+1],j+1)
            det=a*c-b*b
            r1=lax.rsqrt(a); rd=lax.rsqrt(det); r2=r1*rd
            W=a*C[j+1]-b*C[j]
            s1=r1*r1; s2=r2*r2
            L1=C[j]*r1; L2=W*r2
            c1={k:row(C[j],k) for k in range(j+1,8)}
            w2={k:row(W,k) for k in range(j+2,8)}
            l1={k:c1[k]*r1 for k in c1}; l2={k:w2[k]*r2 for k in w2}
            for k in range(j+2,8):
                if k<j+4: C[k]=(C[k]-(C[j]*c1[k])*s1)-(W*w2[k])*s2
                else: C[k]=(C[k]-L1*l1[k])-L2*l2[k]
            g=a*r2
            res=[]
            for V in (VA,VX):
                v0=row(V,j); v1=row(V,j+1)
                res.append((v0*r1,(a*v1-b*v0)*r2))
            (A0,A1),(X0,X1)=res
            RX+= [X0,X1]
            oA=jnp.where(sub==j,A0,jnp.where(sub==j+1,A1,oA))
            oX=jnp.where(sub==j,X0,jnp.where(sub==j+1,X1,oX))
            if j<6:
                L1m=jnp.where(sub>j+1,L1,0.0); L2m=jnp.where(sub>j+1,L2,0.0)
                VA=VA-L1m*A0-L2m*A1
                VX=VX-L1m*X0-L2m*X1
            for q in Q:
                q0=Q[q][j]*r1
                q1=(Q[q][j+1]-q0*l1[j+1])*g
                LQ[q]+=[q0,q1]
                for k in range(j+2,8): Q[q][k]=Q[q][k]-q0*l1[k]-q1*l2[k]
        R.append(jnp.where(lane<lo+8,oA,oX)); I.append(oX)
        if p<15:
            for q in Q:
                t=jnp.where(inpan,0.0,T[q])
                for j in range(8): t=t-LQ[q][j]*RX[j]
                T[q]=t
            if slide:
                for k in range(8):
                    t=Cn[k]
                    for j in range(8): t=t-LQ[p+1][j]*row(LQ[p+1][j],k)
                    Cn[k]=t
                C=Cn
            else: C=[col(T[p+1],lo+8+c) for c in range(8)]
    return R,I
BF=jnp.bfloat16
def split3(x):
    h=x.astype(BF).astype(F32); r=x-h; m=r.astype(BF).astype(F32); l=r-m
    return h,m,l
def outer6(xs,lo,lane):
    n=len(xs)
    x=jnp.concatenate(xs,axis=0)
    z=jnp.concatenate([t if i==n-1 else jnp.where((lane>=lo-8*(n-2-i))&(lane<lo+8),0.0,t) for i,t in enumerate(xs)],axis=0)
    h,m,l=split3(x); zh,zm,zl=split3(z)
    a=jnp.concatenate([h,h,m,m,h,l],axis=0)
    b=jnp.concatenate([zh,zm,zh,zm,zl,zh],axis=0).astype(BF)
    return jnp.dot(a.T.astype(BF),b,preferred_element_type=F32)
def factor_inplace2(T,G=3,B=2):
    T=list(T)
    sub=lax.broadcasted_iota(jnp.int32,(8,128),0); lane=lax.broadcasted_iota(jnp.int32,(8,128),1)
    R=[];I=[]
    C=[col(T[0],c) for c in range(8)]
    for p in range(16):
        lo=8*p
        inpan=(lane>=lo)&(lane<lo+8); inbat=(lane>=lo-8*(p%B))&(lane<lo+8)
        VA=T[p]
        VX=jnp.where(inpan,jnp.where(lane==sub+lo,1.0,0.0),T[p])
        end=min(p-p%B+B+G,16); near=range(p+1,end); far=range(end,16) if p%B==B-1 else ()
        Q={q:[col(T[q],lo+c) for c in range(8)] for q in near}
        Cn=[col(T[p+1],lo+8+c) for c in range(8)] if p<15 else None
        LQ={q:[] for q in near}; RX=[]
        oA=jnp.zeros((8,128),F32); oX=jnp.zeros((8,128),F32)
        for j in (0,2,4,6):
            a=row(C[j],j); b=row(C[j],j+1); c=row(C[j+1],j+1)
            det=a*c-b*b
            r1=lax.rsqrt(a); rd=lax.rsqrt(det); r2=r1*rd
            W=a*C[j+1]-b*C[j]
            s1=r1*r1; s2=r2*r2
            L1=C[j]*r1; L2=W*r2
            c1={k:row(C[j],k) for k in range(j+1,8)}
            w2={k:row(W,k) for k in range(j+2,8)}
            l1={k:c1[k]*r1 for k in c1}; l2={k:w2[k]*r2 for k in w2}
            for k in range(j+2,8):
                if k<j+4: C[k]=(C[k]-(C[j]*c1[k])*s1)-(W*w2[k])*s2
                else: C[k]=(C[k]-L1*l1[k])-L2*l2[k]
            g=a*r2
            res=[]
            for V in (VA,VX):
                v0=row(V,j); v1=row(V,j+1)
                res.append((v0*r1,(a*v1-b*v0)*r2))
            (A0,A1),(X0,X1)=res
            RX+= [X0,X1]
            oA=jnp.where(sub==j,A0,jnp.where(sub==j+1,A1,oA))
            oX=jnp.where(sub==j,X0,jnp.where(sub==j+1,X1,oX))
            if j<6:
                L1m=jnp.where(sub>j+1,L1,0.0); L2m=jnp.where(sub>j+1,L2,0.0)
                VA=VA-L1m*A0-L2m*A1
                VX=VX-L1m*X0-L2m*X1
            for q in Q:
                q0=Q[q][j]*r1
                q1=(Q[q][j+1]-q0*l1[j+1])*g
                LQ[q]+=[q0,q1]
                for k in range(j+2,8): Q[q][k]=Q[q][k]-q0*l1[k]-q1*l2[k]
        R.append(jnp.where(lane<lo+8,oA,oX)); I.append(oX)
        if p<15:
            if len(far):
                D=outer6(I[-B:],lo,lane)
            for q in near:
                t=jnp.where(inpan,0.0,T[q])
                for j in range(8): t=t-LQ[q][j]*RX[j]
                T[q]=t
            for k in range(8):
                t=Cn[k]
                for j in range(8): t=t-LQ[p+1][j]*row(LQ[p+1][j],k)
                Cn[k]=t
            C=Cn
            for q in far:
                T[q]=jnp.where(inbat,0.0,T[q])-D[8*q:8*q+8,:]
    return R,I
MESH=pl.DeviceIdType.MESH
NS=1024; CAP=4096; ROWS=4608; SLABS=(512,512,1024,1024,1024)
PIECES=((0,512,(0,1,2)),(512,512,(1,2,0)),(1024,512,(2,0,1)),(1536,1024,(0,1,2)),(2560,1024,(1,2,0)),(3584,1024,(2,0,1)))
HALF=[n//2 for _,n,_ in PIECES]
def split3b(x):
    h=x.astype(BF); r=x-h.astype(F32); m=r.astype(BF); l=(r-m.astype(F32)).astype(BF)
    return h,m,l
def lhs6(x):
    h,m,l=split3b(x); return jnp.concatenate([h,h,m,m,h,l],axis=1)
def rhs6(x):
    h,m,l=split3b(x); return jnp.concatenate([h,m,h,m,l,h],axis=0)
def brow(k,j): return 128*(8*k-k*(k-1)//2+(j-k))
def blk(k,j): return pl.ds(brow(k,j),128)

def gram_part(cnt_ref,pi_ref,x_hbm,v_ref,pr_ref,g,info,xb,xsem):
    cps=[]; at=0
    for i,n in enumerate(SLABS):
        cp=pltpu.make_async_copy(x_hbm.at[pl.ds(at,n)],xb.at[pl.ds(at,n)],xsem.at[i]); cp.start()
        cps.append((cp,at,n)); at+=n
    def accum(first,lhs,rhs,v):
        Dv=jnp.dot(v,rhs,preferred_element_type=F32)
        for j in range(8):
            dv=Dv[0:1,128*j:128*j+128]
            info[j:j+1,:]=dv if first else info[j:j+1,:]+dv
        for c in range(4):
            D=lax.dot_general(lhs[:,:256*(c+1)],rhs[:,256*c:256*c+256],(((0,),(0,)),((),())),preferred_element_type=F32)
            for u in range(2):
                j=2*c+u
                for i in range(j+1):
                    d=D[128*i:128*i+128,128*u:128*u+128]
                    g[blk(i,j),:]=d if first else g[blk(i,j),:]+d
    sub=lax.broadcasted_iota(jnp.int32,(8,128),0)
    pv=jnp.zeros((8,128),F32)
    for i in range(8): pv=jnp.where(sub==i,pi_ref[i],pv)
    h,m,l=split3(jnp.concatenate([pr_ref[...],pv],axis=1))
    z=jnp.zeros((80,NS+128),F32)
    pa=jnp.concatenate([h,h,m,m,h,l,z],axis=0)
    pb=jnp.concatenate([h,m,h,m,l,h,z],axis=0)[:,:NS].astype(BF)
    accum(True,pa[:,:NS].astype(BF),pb,pa[:,NS:].T[:16].astype(BF))
    for cp,at,n in cps:
        cp.wait()
        x=xb[pl.ds(at,n),:]
        xm=jnp.where(lax.broadcasted_iota(jnp.int32,(n,NS),0)+at<cnt_ref[0],x,jnp.zeros((),BF))
        vf=v_ref[at//128:(at+n)//128,:].astype(F32)
        v=jnp.broadcast_to(jnp.concatenate([vf[i:i+1,:] for i in range(n//128)],axis=1),(16,n)).astype(BF)
        accum(False,x,xm,v)
    eye=lax.broadcasted_iota(jnp.int32,(128,128),0)==lax.broadcasted_iota(jnp.int32,(128,128),1)
    lane=lax.broadcasted_iota(jnp.int32,(1,128),1)
    for k in range(8):
        dg=jnp.sum(jnp.where(eye,g[blk(k,k),:],0.0),axis=0,keepdims=True)
        for base,r in ((64,info[k:k+1,:]),(80,dg)):
            rr=pltpu.roll(jnp.broadcast_to(r,(8,128)),64,1)[0:1,:]
            g[base+2*k:base+2*k+1,:]=jnp.where(lane<64,r,g[base+2*k:base+2*k+1,:])
            g[base+2*k+1:base+2*k+2,:]=jnp.where(lane<64,rr,g[base+2*k+1:base+2*k+2,:])

class Comm:
    def __init__(self,g,a,r0,r1,r2,p0,p1,p2,ssem,rsem):
        self.__dict__.update(g=g,a=a,r0=r0,r1=r1,r2=r2,p0=p0,p1=p1,p2=p2,ssem=ssem,rsem=rsem)
        f=lax.axis_index("fibre"); q=lax.axis_index("blk")
        self.core=f%2; self.co=(q//4,q%4,f//2); self.q=q; self.n=0; self.fly={}
        self.partner=(self.co[2]*2+(1-self.core),q)
    def peer(self,dim,d):
        c=list(self.co); c[dim]=(c[dim]+d)%4
        return (c[2]*2+self.core,c[0]*4+c[1])
    def greet(self):
        bar=pltpu.get_barrier_semaphore()
        pl.semaphore_signal(bar,inc=1,device_id=self.partner,device_id_type=MESH)
        for dim in range(3):
            for d in range(1,4):
                pl.semaphore_signal(bar,inc=1,device_id=self.peer(dim,d),device_id_type=MESH)
    def met(self): pl.semaphore_wait(pltpu.get_barrier_semaphore(),10)
    def send(self,src,dst,dev):
        i=self.n; self.n+=1
        c=pltpu.make_async_remote_copy(src_ref=src,dst_ref=dst,send_sem=self.ssem.at[i],recv_sem=self.rsem.at[i],device_id=dev,device_id_type=MESH)
        c.start(); return c
    def off(self,c,lvl):
        b,_,dims=PIECES[c]; h=HALF[c]
        o=b+self.core*h
        if lvl>=1: o=o+self.co[dims[0]]*(h//4)
        if lvl>=2: o=o+self.co[dims[1]]*(h//16)
        return pl.multiple_of(o,8)
    def step(self,n,cs):
        al=lambda v: pl.multiple_of(v,8)
        for c in cs:
            b,_,dims=PIECES[c]; h=HALF[c]; h4=h//4; h16=h//16
            if n==5 and c<3: continue
            for x in self.fly.pop(c,()): x.wait()
            core,co=self.core,self.co
            if n==0:
                out=[self.send(self.g.at[pl.ds(al(b+(1-core)*h),h)],self.r0[c],self.partner)]
            elif n==1:
                self.p0[c][...]=self.g[pl.ds(al(b+core*h),h),:]+self.r0[c][...]
                out=[self.send(self.p0[c].at[pl.ds(al(((co[dims[0]]+d)%4)*h4),h4)],self.r1[c].at[d-1],self.peer(dims[0],d)) for d in (2,1,3)]
            elif n==2 and c<3:
                r=self.r1[c]; me=co[dims[1]]
                self.r2[c][me]=(self.p0[c][pl.ds(al(co[dims[0]]*h4),h4),:]+r[0])+(r[1]+r[2])
                out=[self.send(self.r2[c].at[me],self.r2[c].at[me],self.peer(dims[1],d)) for d in (2,1,3)]
            elif n==3 and c<3:
                t=self.r2[c]; me=co[dims[2]]
                self.p2[c][me]=(t[0]+t[1])+(t[2]+t[3])
                out=[self.send(self.p2[c].at[me],self.p2[c].at[me],self.peer(dims[2],d)) for d in (2,1,3)]
            elif n==4 and c<3:
                s=pl.ds(self.off(c,1),h4); t=self.p2[c]
                self.a[s,:]=(t[0]+t[1])+(t[2]+t[3])
                out=[self.send(self.a.at[s],self.a.at[s],self.peer(dims[0],d)) for d in (2,1,3)]
            elif n==2:
                r=self.r1[c]
                self.p1[c][...]=(self.p0[c][pl.ds(al(co[dims[0]]*h4),h4),:]+r[0])+(r[1]+r[2])
                out=[self.send(self.p1[c].at[pl.ds(al(((co[dims[1]]+d)%4)*h16),h16)],self.r2[c].at[d-1],self.peer(dims[1],d)) for d in (2,1,3)]
            elif n==3:
                r=self.r2[c]; me=co[dims[2]]
                self.p2[c][me]=(self.p1[c][pl.ds(al(co[dims[1]]*h16),h16),:]+r[0])+(r[1]+r[2])
                out=[self.send(self.p2[c].at[me],self.p2[c].at[me],self.peer(dims[2],d)) for d in (2,1,3)]
            elif n==4:
                s=pl.ds(self.off(c,2),h16); t=self.p2[c]
                self.a[s,:]=(t[0]+t[1])+(t[2]+t[3])
                out=[self.send(self.a.at[s],self.a.at[s],self.peer(dims[1],d)) for d in (2,1,3)]
            elif n==5:
                s=pl.ds(self.off(c,1),h4)
                out=[self.send(self.a.at[s],self.a.at[s],self.peer(dims[0],d)) for d in (2,1,3)]
            elif n==6:
                s=pl.ds(self.off(c,0),h)
                out=[self.send(self.a.at[s],self.a.at[s],self.partner)]
            else: out=[]
            self.fly[c]=out

def body(cnt_ref,pi_ref,x_hbm,v_ref,pr_ref,o_ref,y_ref,xb,xsem,g,info,a,A,Rs,Li,Xs,Ys,*scr):
    k6=lambda i: scr[6*i:6*i+6]
    cm=Comm(g,a,k6(0),k6(1),k6(2),k6(3),k6(4),k6(5),scr[36],scr[37])
    cm.greet()
    gram_part(cnt_ref,pi_ref,x_hbm,v_ref,pr_ref,g,info,xb,xsem)
    rest(cm,o_ref,y_ref,a,A,Rs,Li,Xs,Ys)

def rest(cm,o_ref,y_ref,a,A,Rs,Li,Xs,Ys):
    P0=(0,1,2); P1=(3,4,5)
    cm.met()
    for n,cs in ((0,P0),(0,P1),(1,P0),(1,P1),(2,P0),(2,P1),(3,P0),(3,P1),(4,P0),(4,P1),(6,P0),(5,P1),(7,P0)): cm.step(n,cs)
    ii=lax.broadcasted_iota(jnp.int32,(8,128),0); jj=lax.broadcasted_iota(jnp.int32,(8,128),1)
    big=(128,128)
    l16=lax.broadcasted_iota(jnp.int32,(16,128),1)
    def unpack(base):
        e=a[base:base+16,:]; er=pltpu.roll(e,64,1)
        return [jnp.where(l16[:1]<64,e[2*k:2*k+1,:],er[2*k+1:2*k+2,:]) for k in range(8)]
    dg=unpack(80); dr=[lax.rsqrt(d) for d in dg]
    bl=[b*d for b,d in zip(unpack(64),dr)]
    a00=a[0:128,:]
    low=(lax.broadcasted_iota(jnp.int32,big,0)>=64)&(lax.broadcasted_iota(jnp.int32,big,1)<64)
    dc=[bc(d,big).T for d in dr]
    A[0:128,:]=jnp.where(low,a00.T,a00)*dc[0]*dr[0]
    def scale(k,j): A[blk(k,j),:]=a[blk(k,j),:]*dc[k]*dr[j]
    for j in range(1,8): scale(0,j)
    for j in range(1,5): scale(1,j)
    def factor(k):
        o=brow(k,k)
        R,I=factor_inplace2(G=1,B=5,T=[A[o+8*p:o+8*p+8,:] for p in range(16)])
        for p in range(16):
            Rs[128*k+8*p:128*k+8*p+8,128*k:128*k+128]=jnp.where(jj>=ii+8*p,R[p],0.0)
            Li[8*p:8*p+8,:]=jnp.where(jj<8*p+8,I[p],0.0)
        if k: Rs[128*k:128*k+128,:128*k]=jnp.zeros((128,128*k),F32)
    def panel(k):
        Linv=Li[...]
        bk=jnp.concatenate([bl[k],jnp.zeros((7,128),F32)],axis=0)
        yk=lax.dot_general(bk,Linv,(((1,),(1,)),((),())),precision=lax.Precision.HIGHEST,preferred_element_type=F32)
        y_ref[k:k+1,:]=yk[0:1,:]
        n=7-k
        if n==0: return
        row_=jnp.concatenate([A[blk(k,j),:] for j in range(k+1,8)],axis=1)
        Rk=jnp.dot(lhs6(Linv),rhs6(row_),preferred_element_type=F32)
        Rs[128*k:128*k+128,128*(k+1):]=Rk
        Xs[0:16,:]=lhs6(jnp.concatenate([yk,jnp.zeros((8,128),F32)],axis=0))
        for i in range(n): Xs[16+128*i:144+128*i,:]=lhs6(Rk[:,128*i:128*i+128].T)
        Ys[:,:128*n]=rhs6(Rk)
    def update(k,j0,j1,i0,i1,withb):
        lo=0 if withb else 16+128*(i0-k-1)
        if withb and i0>k+1: X=jnp.concatenate([Xs[0:16,:],Xs[16+128*(i0-k-1):16+128*(i1-k-1),:]],axis=0)
        else: X=Xs[lo:16+128*(i1-k-1),:]
        D=jnp.dot(X,Ys[:,128*(j0-k-1):128*(j1-k-1)],preferred_element_type=F32)
        b0=16 if withb else 0
        for j in range(j0,j1):
            u=128*(j-j0)
            if withb: bl[j]=bl[j]-D[0:1,u:u+128]
            for i in range(i0,min(i1,j+1)):
                z=b0+128*(i-i0)
                A[blk(i,j),:]=A[blk(i,j),:]-D[z:z+128,u:u+128]
    factor(0)
    panel(0)
    update(0,1,5,1,2,True)
    cm.step(6,P1)
    factor(1)
    cm.step(7,P1)
    for k in range(1,8):
        for j in range(max(k,5) if k==1 else k,8): scale(k,j)
    update(0,5,8,1,8,True)
    update(0,2,3,2,3,False)
    update(0,3,5,2,5,False)
    for k in range(1,8):
        panel(k)
        if k==7: break
        for j in range(k+1,8,2): update(k,j,min(j+2,8),k+1,min(j+2,8),True)
        factor(k+1)
    s=pl.multiple_of(cm.q*64,64)
    for j in range(8):
        o_ref[:,128*j:128*j+128]=Rs[pl.ds(s,64),128*j:128*j+128]*(dg[j]*dr[j])

def finish(o_in,y_in,o_ref,y_ref):
    o_ref[...]=o_in[...]
    y_ref[...]=y_in[...]

def local(readings,values,counts,prior_root,prior_info):
    V=lambda *s: pltpu.VMEM(s,F32)
    H=HALF
    scr=[pltpu.VMEM((CAP,NS),BF),pltpu.SemaphoreType.DMA((len(SLABS),))]
    scr+=[V(ROWS,128),V(8,128),V(ROWS,128),V(ROWS,128),V(NS,NS),V(128,128),pltpu.VMEM((16+7*128,768),BF),pltpu.VMEM((768,896),BF)]
    scr+=[V(h,128) for h in H]+[V(3,h//4,128) for h in H]+[V(4,h//4,128) if i<3 else V(3,h//16,128) for i,h in enumerate(H)]+[V(h,128) for h in H]+[V(h//4,128) for h in H]+[V(4,h//4 if i<3 else h//16,128) for i,h in enumerate(H)]
    scr+=[pltpu.SemaphoreType.DMA((102,)),pltpu.SemaphoreType.DMA((102,))]
    smem=pl.BlockSpec(memory_space=pltpu.SMEM); vmem=pl.BlockSpec(memory_space=pltpu.VMEM)
    outs=(jax.ShapeDtypeStruct((64,NS),F32),jax.ShapeDtypeStruct((8,128),F32))
    root,y=pl.pallas_call(body,
        in_specs=[smem,smem,pl.BlockSpec(memory_space=pl.ANY),vmem,vmem],
        out_specs=(vmem,vmem),out_shape=outs,scratch_shapes=scr,
        compiler_params=pltpu.CompilerParams(collective_id=0,has_side_effects=True,vmem_limit_bytes=58*2**20),
    )(counts,prior_info,readings,values.reshape(CAP//128,128),prior_root)
    root,y=pl.pallas_call(finish,in_specs=[vmem,vmem],out_specs=(vmem,vmem),out_shape=outs)(root,y)
    return root,y.reshape(NS)
from jax.sharding import PartitionSpec as P
def solution(mesh):
    placed=(P(("fibre","blk"),None),P(("fibre","blk")),P(("fibre","blk")),P(("fibre","blk"),None),P(("fibre","blk")))
    return jax.shard_map(local,mesh=mesh,in_specs=placed,out_specs=(P("blk",None),P()),check_vma=False)
```
